32 devices in a mesh: dp: 8 (over y, x, core), tensor: 4 (over z).
Axes of the slice: x: 2, y: 2, z: 4, core: 2. Of those that a mesh axis runs over, the one named last changes fastest.
Arguments:
- tokens: float32 [8192, 768], P(('dp', 'tensor')), may hold values from -6 to 6
- conditioning: float32 [32, 768], P('dp'), may hold values from -6 to 6
- cotangent: float32 [8192, 768], P(('dp', 'tensor')), may hold values from -6 to 6
- w_ada: bfloat16 [768, 4608], P('dp', 'tensor'), may hold values from -0.21875 to 0.21875
- b_ada: float32 [4608], P('tensor'), may hold values from -3 to 3
- w_qkv: bfloat16 [768, 3, 768], P('dp', None, 'tensor'), may hold values from -0.21875 to 0.21875
- b_qv: float32 [2, 768], P(None, 'tensor'), may hold values from -3 to 3
- w_out: bfloat16 [768, 768], P('tensor', 'dp'), may hold values from -0.75 to 0.75
- b_out: float32 [768], replicated, may hold values from -3 to 3
- w_fc1: bfloat16 [768, 3072], P('dp', 'tensor'), may hold values from -0.21875 to 0.21875
- b_fc1: float32 [3072], P('tensor'), may hold values from -3 to 3
- w_fc2: bfloat16 [3072, 768], P('tensor', 'dp'), may hold values from -0.109375 to 0.109375
- b_fc2: float32 [768], replicated, may hold values from -3 to 3
Outputs:
- output: float32 [8192, 768], P(('dp', 'tensor'))
- grad_tokens: float32 [8192, 768], P(('dp', 'tensor'))
- grad_cond: float32 [32, 768], P('dp')
- grad_w_ada: float32 [768, 4608], P('dp', 'tensor')
- grad_b_ada: float32 [4608], P('tensor')
- grad_w_qkv: float32 [768, 3, 768], P('dp', None, 'tensor')
- grad_b_qv: float32 [2, 768], P(None, 'tensor')
- grad_w_out: float32 [768, 768], P('tensor', 'dp')
- grad_b_out: float32 [768], replicated
- grad_w_fc1: float32 [768, 3072], P('dp', 'tensor')
- grad_b_fc1: float32 [3072], P('tensor')
- grad_w_fc2: float32 [3072, 768], P('tensor', 'dp')
- grad_b_fc2: float32 [768], replicated
The draws below stay inside these ranges and needn't reach their ends.
All inputs are finite; a program needn't handle non-finite values.
Results may differ from the reference program's by a relative error of at most 0.015.
The reference program's roundings to bfloat16 on the way count: a program that leaves them out, or rounds other values in their place, can miss the bound.
Values may be sent and summed in bfloat16 or wider, within the bound.
No kernel may reach another device: no remote copies, remote signals or barrier semaphores. Data moves between devices by JAX's collectives and lax.ppermute only.
A program may use at most 128 MiB of HBM per device.

```python
import jax
import jax.numpy as jnp
from jax import lax

D = 768
HEADS = 12
HD = 64
FF = 3072
SEQ = 256
LATENTS = 32
TOKENS = 8192


def levels(own_key, shape, shards, low, top_value):
    factor_of, own = 1.0, jax.random.fold_in(own_key, 6)
    for axis_at, parts in shards:
        steps = jnp.exp(jax.random.uniform(jax.random.fold_in(own, axis_at), (parts,), jnp.float32, low / len(shards), top_value / len(shards)))
        factor_of = factor_of * jnp.repeat(steps, shape[axis_at] // parts).reshape([-1 if axis == axis_at else 1 for axis in range(len(shape))])
    return factor_of


def centred(rng, shape, width, limit, cuts=(), kind=jnp.bfloat16):
    entries = width * jax.random.normal(rng, shape, jnp.float32)
    if cuts:
        entries = entries * levels(rng, shape, cuts, -0.22, 0.18)
    return jnp.clip(entries, -limit, limit).astype(kind)


def setup_inputs(seed: int = 0) -> dict:
    splits = jax.random.split(jax.random.key(seed), 14)
    return {
        "tokens": centred(splits[0], (TOKENS, D), 1.0, 6.0, ((0, 32),), jnp.float32),
        "conditioning": centred(splits[1], (LATENTS, D), 1.0, 6.0, ((0, 8),), jnp.float32),
        "cotangent": centred(splits[2], (TOKENS, D), 1.0, 6.0, ((0, 32),), jnp.float32),
        "w_ada": centred(splits[3], (D, 6 * D), D ** -0.5, 0.21875, ((0, 8), (1, 4))),
        "b_ada": centred(splits[4], (6 * D,), 0.5, 3.0, ((0, 4),), jnp.float32),
        "w_qkv": centred(splits[5], (D, 3, D), D ** -0.5, 0.21875, ((0, 8), (2, 4))),
        "b_qv": centred(splits[6], (2, D), 0.5, 3.0, ((1, 4),), jnp.float32),
        "w_out": centred(splits[7], (D, D), HD ** -0.5, 0.75, ((0, 4), (1, 8))),
        "b_out": centred(splits[8], (D,), 0.5, 3.0, (), jnp.float32),
        "w_fc1": centred(splits[9], (D, FF), D ** -0.5, 0.21875, ((0, 8), (1, 4))),
        "b_fc1": centred(splits[10], (FF,), 0.5, 3.0, ((0, 4),), jnp.float32),
        "w_fc2": centred(splits[11], (FF, D), FF ** -0.5, 0.109375, ((0, 4), (1, 8))),
        "b_fc2": centred(splits[12], (D,), 0.5, 3.0, (), jnp.float32),
    }


epsilon = 1e-06
gelu_coef = 0.7978845608028654
cube_coef = 0.044715
latent_block = 16

def gelu_parts(pre_act):
    inner_arg = gelu_coef * (pre_act + cube_coef * pre_act * pre_act * pre_act)
    tangent = jnp.tanh(inner_arg)
    result = 0.5 * pre_act * (1.0 + tangent)
    gelu_slope = 0.5 * (1.0 + tangent) + 0.5 * pre_act * (1.0 - tangent * tangent) * gelu_coef * (1.0 + 3.0 * cube_coef * pre_act * pre_act)
    return (result, gelu_slope)

def normalize(rows_in):
    center = rows_in - lax.optimization_barrier(jnp.mean(rows_in, axis=-1, keepdims=True))
    inv_std = lax.rsqrt(lax.optimization_barrier(jnp.mean(center * center, axis=-1, keepdims=True)) + epsilon)
    return (center * inv_std, inv_std)

def norm_back(grad_normed, normed, inv_std):
    return inv_std * (grad_normed - lax.optimization_barrier(jnp.mean(grad_normed, axis=-1, keepdims=True)) - normed * lax.optimization_barrier(jnp.mean(grad_normed * normed, axis=-1, keepdims=True)))

def block_pass(weights, tokens, conditioning, cotangent):
    w_ada, b_ada, w_qkv, b_qv, w_out, b_out, w_fc1, b_fc1, w_fc2, b_fc2 = weights
    f32 = jnp.float32
    bf16 = jnp.bfloat16
    latents_here = tokens.shape[0]
    row_count = latents_here * SEQ
    score_scale = HD ** (-0.5)
    sig_cond = jax.nn.sigmoid(conditioning)
    silu_cond = (conditioning * sig_cond).astype(bf16)
    modulation = (jnp.dot(silu_cond, w_ada, preferred_element_type=f32) + b_ada).reshape(latents_here, 6, 1, D)
    shift_one, scale_one, gate_one, shift_two, scale_two, gate_two = [modulation[:, which] for which in range(6)]
    normed_one, inv_one = normalize(tokens)
    hidden_one = (normed_one * (1.0 + scale_one) + shift_one).astype(bf16).reshape(row_count, D)
    projected = jnp.dot(hidden_one, w_qkv.reshape(D, 3 * D), preferred_element_type=f32).reshape(row_count, 3, D)
    queries = (projected[:, 0] + b_qv[0]).astype(bf16).reshape(latents_here, SEQ, HEADS, HD)
    key_rows = projected[:, 1].astype(bf16).reshape(latents_here, SEQ, HEADS, HD)
    values = (projected[:, 2] + b_qv[1]).astype(bf16).reshape(latents_here, SEQ, HEADS, HD)
    scores = jnp.einsum('lqhe,lkhe->lhqk', queries.astype(f32), key_rows.astype(f32)) * score_scale
    row_max = lax.optimization_barrier(jnp.max(scores, axis=-1, keepdims=True))
    log_total = row_max + jnp.log(lax.optimization_barrier(jnp.sum(jnp.exp(scores - row_max), axis=-1, keepdims=True)))
    attn_probs = jnp.exp(scores - log_total)
    probs_low = attn_probs.astype(bf16)
    attended = jnp.einsum('lhqk,lkhe->lqhe', probs_low.astype(f32), values.astype(f32)).astype(bf16).reshape(row_count, D)
    branch_one = jnp.dot(attended, w_out, preferred_element_type=f32).reshape(latents_here, SEQ, D) + b_out
    middle = tokens + gate_one * branch_one
    normed_two, inv_two = normalize(middle)
    hidden_two = (normed_two * (1.0 + scale_two) + shift_two).astype(bf16).reshape(row_count, D)
    pre_act = jnp.dot(hidden_two, w_fc1, preferred_element_type=f32) + b_fc1
    activated, gelu_slope = gelu_parts(pre_act)
    act_low = activated.astype(bf16)
    branch_two = (jnp.dot(act_low, w_fc2, preferred_element_type=f32) + b_fc2).reshape(latents_here, SEQ, D)
    output = middle + gate_two * branch_two
    grad_gate_two = lax.optimization_barrier(jnp.sum(cotangent * branch_two, axis=1))
    grad_branch_two = (cotangent * gate_two).astype(bf16).reshape(row_count, D)
    grad_b_fc2 = lax.optimization_barrier(jnp.sum(grad_branch_two.astype(f32), axis=0))
    grad_w_fc2 = jnp.dot(act_low.T, grad_branch_two, preferred_element_type=f32)
    grad_pre = jnp.dot(grad_branch_two, w_fc2.T, preferred_element_type=f32) * gelu_slope
    grad_b_fc1 = lax.optimization_barrier(jnp.sum(grad_pre, axis=0))
    grad_pre_low = grad_pre.astype(bf16)
    grad_w_fc1 = jnp.dot(hidden_two.T, grad_pre_low, preferred_element_type=f32)
    grad_hidden_two = jnp.dot(grad_pre_low, w_fc1.T, preferred_element_type=f32).reshape(latents_here, SEQ, D)
    grad_shift_two = lax.optimization_barrier(jnp.sum(grad_hidden_two, axis=1))
    grad_scale_two = lax.optimization_barrier(jnp.sum(grad_hidden_two * normed_two, axis=1))
    grad_middle = cotangent + norm_back(grad_hidden_two * (1.0 + scale_two), normed_two, inv_two)
    grad_gate_one = lax.optimization_barrier(jnp.sum(grad_middle * branch_one, axis=1))
    grad_branch_one = (grad_middle * gate_one).astype(bf16).reshape(row_count, D)
    grad_b_out = lax.optimization_barrier(jnp.sum(grad_branch_one.astype(f32), axis=0))
    grad_w_out = jnp.dot(attended.T, grad_branch_one, preferred_element_type=f32)
    grad_attended = jnp.dot(grad_branch_one, w_out.T, preferred_element_type=f32).astype(bf16).reshape(latents_here, SEQ, HEADS, HD)
    grad_values = jnp.einsum('lhqk,lqhe->lkhe', probs_low.astype(f32), grad_attended.astype(f32))
    grad_probs = jnp.einsum('lqhe,lkhe->lhqk', grad_attended.astype(f32), values.astype(f32))
    inner_sum = lax.optimization_barrier(jnp.sum(attn_probs * grad_probs, axis=-1, keepdims=True))
    grad_scores = (attn_probs * (grad_probs - inner_sum) * score_scale).astype(bf16)
    grad_queries = jnp.einsum('lhqk,lkhe->lqhe', grad_scores.astype(f32), key_rows.astype(f32)).reshape(row_count, D)
    grad_keys = jnp.einsum('lhqk,lqhe->lkhe', grad_scores.astype(f32), queries.astype(f32)).reshape(row_count, D)
    grad_values = grad_values.reshape(row_count, D)
    grad_b_qv = jnp.stack([lax.optimization_barrier(jnp.sum(grad_queries, axis=0)), lax.optimization_barrier(jnp.sum(grad_values, axis=0))])
    grad_proj = jnp.stack([grad_queries, grad_keys, grad_values], axis=1).astype(bf16).reshape(row_count, 3 * D)
    grad_w_qkv = jnp.dot(hidden_one.T, grad_proj, preferred_element_type=f32).reshape(D, 3, D)
    grad_hidden_one = jnp.dot(grad_proj, w_qkv.reshape(D, 3 * D).T, preferred_element_type=f32).reshape(latents_here, SEQ, D)
    grad_shift_one = lax.optimization_barrier(jnp.sum(grad_hidden_one, axis=1))
    grad_scale_one = lax.optimization_barrier(jnp.sum(grad_hidden_one * normed_one, axis=1))
    grad_tokens = grad_middle + norm_back(grad_hidden_one * (1.0 + scale_one), normed_one, inv_one)
    grad_mod = jnp.stack([grad_shift_one, grad_scale_one, grad_gate_one, grad_shift_two, grad_scale_two, grad_gate_two], axis=1).reshape(latents_here, 6 * D)
    grad_b_ada = lax.optimization_barrier(jnp.sum(grad_mod, axis=0))
    grad_w_ada = jnp.dot(silu_cond.astype(f32).T, grad_mod, precision=lax.Precision.HIGHEST)
    grad_silu = jnp.dot(grad_mod, w_ada.astype(f32).T, precision=lax.Precision.HIGHEST)
    grad_cond = grad_silu * sig_cond * (1.0 + conditioning * (1.0 - sig_cond))
    grads = (grad_w_ada, grad_b_ada, grad_w_qkv, grad_b_qv, grad_w_out, grad_b_out, grad_w_fc1, grad_b_fc1, grad_w_fc2, grad_b_fc2)
    return (output, grad_tokens, grad_cond, grads)

def reference(tokens, conditioning, cotangent, w_ada, b_ada, w_qkv, b_qv, w_out, b_out, w_fc1, b_fc1, w_fc2, b_fc2):
    weights = (w_ada, b_ada, w_qkv, b_qv, w_out, b_out, w_fc1, b_fc1, w_fc2, b_fc2)
    total_latents = conditioning.shape[0]
    block_count = total_latents // latent_block
    tok_blocks = tokens.reshape(block_count, latent_block, SEQ, D)
    cond_blocks = conditioning.reshape(block_count, latent_block, D)
    cot_blocks = cotangent.reshape(block_count, latent_block, SEQ, D)
    zero_grads = jax.tree.map(lambda member: jnp.zeros(member.shape, jnp.float32), weights)

    def one_step(running, block_inputs):
        block_out, grad_tok, grad_con, grads = block_pass(weights, *block_inputs)
        return (jax.tree.map(jnp.add, running, grads), (block_out, grad_tok, grad_con))
    summed, (outs_all, grad_toks, grad_conds) = lax.scan(one_step, zero_grads, (tok_blocks, cond_blocks, cot_blocks))
    output = outs_all.reshape(total_latents * SEQ, D)
    grad_tokens = grad_toks.reshape(total_latents * SEQ, D)
    grad_cond = grad_conds.reshape(total_latents, D)
    return (output, grad_tokens, grad_cond, summed[0], summed[1], summed[2], summed[3], summed[4], summed[5], summed[6], summed[7], summed[8], summed[9])
```

```python
import jax
import jax.numpy as jnp
from jax import lax
from jax.sharding import PartitionSpec as P

D = 768
HD = 64
SEQ = 256


epsilon = 1e-06
gelu_coef = 0.7978845608028654
cube_coef = 0.044715
f32 = jnp.float32
bf16 = jnp.bfloat16
BOTH = ("dp", "tensor")


def gelu_parts(pre_act):
    inner_arg = gelu_coef * (pre_act + cube_coef * pre_act * pre_act * pre_act)
    tangent = jnp.tanh(inner_arg)
    result = 0.5 * pre_act * (1.0 + tangent)
    gelu_slope = 0.5 * (1.0 + tangent) + 0.5 * pre_act * (1.0 - tangent * tangent) * gelu_coef * (
        1.0 + 3.0 * cube_coef * pre_act * pre_act
    )
    return (result, gelu_slope)


def normalize(rows_in):
    center = rows_in - jnp.mean(rows_in, axis=-1, keepdims=True)
    inv_std = lax.rsqrt(jnp.mean(center * center, axis=-1, keepdims=True) + epsilon)
    return (center * inv_std, inv_std)


def norm_back(grad_normed, normed, inv_std):
    return inv_std * (
        grad_normed
        - jnp.mean(grad_normed, axis=-1, keepdims=True)
        - normed * jnp.mean(grad_normed * normed, axis=-1, keepdims=True)
    )


def barrier(*values):
    return lax.optimization_barrier(values)


def swap_dp(value, bit):
    size = lax.axis_size("dp")
    return lax.ppermute(value, "dp", [(i, i ^ bit) for i in range(size)])


def swap_tensor(value, bit):
    size = lax.axis_size("tensor")
    return lax.ppermute(value, "tensor", [(i, i ^ bit) for i in range(size)])


def feature_order(block):
    me = lax.axis_index("dp")
    place = lax.broadcasted_iota(jnp.int32, (D, D), 1)
    source = lax.broadcasted_iota(jnp.int32, (D, D), 0)
    slot = place // block
    flip = ((slot // 2) % 2) * 4 + (slot % 2) * 2 + slot // 4
    return ((me ^ flip) * block + place % block == source).astype(f32)


def spread_z(chunk):
    return [chunk] + [swap_tensor(chunk, j) for j in (1, 2, 3)]


def natural_z(blocks):
    me = lax.axis_index("tensor")
    stacked = jnp.stack(blocks)
    return jnp.stack(
        [lax.dynamic_index_in_dim(stacked, me ^ t, 0, keepdims=False) for t in range(4)]
    )


def gather_first(full):
    low, high = full[:2], full[2:]
    return (low, high, swap_dp(low, 2), swap_dp(high, 4))


def gather_second(low, high, low_got, high_got):
    low_x = jnp.stack([low, low_got], axis=1)
    high_y = jnp.stack([high, high_got], axis=1)
    return (low_x, high_y, swap_dp(low_x, 4), swap_dp(high_y, 2))


def gather_third(low_x, high_y, low_got, high_got):
    low_all = jnp.stack([low_x, low_got], axis=1)
    high_all = jnp.stack([high_y, high_got], axis=2)
    mine = jnp.concatenate([low_all, high_all], axis=0)
    return mine, swap_dp(mine, 1)


def flat_chunk(mine, other):
    parts, _, _, rows, cols = mine.shape
    return jnp.concatenate(
        [mine.reshape(parts, 4 * rows, cols), other.reshape(parts, 4 * rows, cols)], axis=1
    )


def gather_custom(chunk_a, chunk_b, chunk_c):
    za = spread_z(chunk_a)
    za, chunk_b = barrier(za, chunk_b)
    zb = spread_z(chunk_b)
    one_a = gather_first(natural_z(za))
    zb, one_a, chunk_c = barrier(zb, one_a, chunk_c)
    zc = spread_z(chunk_c)
    two_a = gather_second(*one_a)
    one_b = gather_first(natural_z(zb))
    zc, two_a, one_b = barrier(zc, two_a, one_b)
    three_a = gather_third(*two_a)
    two_b = gather_second(*one_b)
    one_c = gather_first(natural_z(zc))
    three_a, two_b, one_c = barrier(three_a, two_b, one_c)
    three_b = gather_third(*two_b)
    two_c = gather_second(*one_c)
    three_b, two_c = barrier(three_b, two_c)
    three_c = gather_third(*two_c)
    return flat_chunk(*three_a), flat_chunk(*three_b), flat_chunk(*three_c)


def scatter_custom(grad_of):
    half = D // 2
    rows = half // 4
    away = swap_dp(grad_of(half, D).astype(bf16), 1)
    mine = grad_of(0, half) + away.astype(f32)
    cols = mine.shape[-1]
    mine = mine.reshape(4, 2, 2, rows, cols)
    low = mine[:2, :, 0] + swap_dp(mine[:2, :, 1].astype(bf16), 2).astype(f32)
    high = mine[2:, 0] + swap_dp(mine[2:, 1].astype(bf16), 4).astype(f32)
    low = low[:, 0] + swap_dp(low[:, 1].astype(bf16), 4).astype(f32)
    high = high[:, 0] + swap_dp(high[:, 1].astype(bf16), 2).astype(f32)
    both = jnp.concatenate([low, high], axis=0)
    me = lax.axis_index("tensor")
    total = lax.dynamic_index_in_dim(both, me, 0, keepdims=False)
    for j in (1, 2, 3):
        part = lax.dynamic_index_in_dim(both, me ^ j, 0, keepdims=False).astype(bf16)
        total = total + swap_tensor(part, j).astype(f32)
    return total


def gather_plain(*chunks):
    full = []
    for chunk in chunks:
        near = lax.all_gather(chunk, "tensor", axis=0)
        full.append(lax.all_gather(near, "dp", axis=1, tiled=True))
    return full


def scatter_plain(grad_of):
    grad = grad_of(0, D)
    near = lax.psum_scatter(grad, "tensor", scatter_dimension=0, tiled=True)[0]
    return lax.psum_scatter(near, "dp", scatter_dimension=0, tiled=True)


def body(
    tokens,
    conditioning,
    cotangent,
    w_ada,
    b_ada,
    w_qkv,
    b_qv,
    w_out,
    b_out,
    w_fc1,
    b_fc1,
    w_fc2,
    b_fc2,
):
    n_d = lax.axis_size("dp")
    n_t = lax.axis_size("tensor")
    devices = n_d * n_t
    dp_at = lax.axis_index("dp")
    t_at = lax.axis_index("tensor")
    custom = n_d == 8 and n_t == 4
    block = w_fc1.shape[0]
    width = w_qkv.shape[2]
    heads_t = width // HD
    ada_cols = w_ada.shape[1]
    group = conditioning.shape[0]
    score_scale = HD ** (-0.5)
    exact = lax.Precision.HIGHEST

    if custom:
        order = feature_order(block)
        shuffle = lambda v: jnp.dot(v, order, precision=exact)
        restore = lambda v: lax.dot_general(v, order, (((1,), (1,)), ((), ())), precision=exact)
        gather, scatter = gather_custom, scatter_custom
    else:
        shuffle = restore = lambda v: v
        gather, scatter = gather_plain, scatter_plain

    chunk_a = jnp.concatenate([w_qkv.reshape(block, 3 * width), w_out.T], axis=1)
    full_a, full_b, full_c = gather(chunk_a, w_fc1, w_fc2.T)
    qkv_t = full_a[:, :, : 3 * width]
    out_t = full_a[:, :, 3 * width :]

    sig_cond = jax.nn.sigmoid(conditioning)
    silu_cond = (conditioning * sig_cond).astype(bf16)
    silu_send = silu_cond.reshape(group, n_d, block).transpose(1, 0, 2)
    silu_rows = lax.all_to_all(silu_send, "dp", split_axis=0, concat_axis=0, tiled=True)
    silu_rows = silu_rows.reshape(n_d * group, block)
    mod_part = jnp.dot(silu_rows, w_ada, preferred_element_type=f32)
    mod_part = mod_part + (dp_at == 0).astype(f32) * b_ada
    mod_got = lax.all_to_all(mod_part, BOTH, split_axis=0, concat_axis=0, tiled=True)
    modulation = jnp.sum(mod_got.reshape(n_d, n_t * ada_cols), axis=0).reshape(6, D)
    modulation = shuffle(modulation)
    shift_one, scale_one, gate_one, shift_two, scale_two, gate_two = [
        modulation[which][None] for which in range(6)
    ]
    b_out_s, b_fc2_s = [row[None] for row in shuffle(jnp.stack([b_out, b_fc2]))]
    bias_full = lax.all_gather(
        jnp.concatenate([b_qv.reshape(-1), b_fc1]), "tensor", axis=0
    )
    b_q = bias_full[:, None, :width]
    b_v = bias_full[:, None, width : 2 * width]
    b_fc1_t = bias_full[:, None, 2 * width :]

    tokens_s = shuffle(tokens)
    cot = shuffle(cotangent)
    normed_one, inv_one = normalize(tokens_s)
    hidden_one = (normed_one * (1.0 + scale_one) + shift_one).astype(bf16)
    projected = jnp.einsum("rd,tdc->trc", hidden_one, qkv_t, preferred_element_type=f32)

    def heads(value):
        return (
            value.reshape(n_t, SEQ, heads_t, HD)
            .transpose(0, 2, 1, 3)
            .reshape(n_t * heads_t, SEQ, HD)
        )

    def unheads(value):
        return (
            value.reshape(n_t, heads_t, SEQ, HD).transpose(0, 2, 1, 3).reshape(n_t, SEQ, width)
        )

    queries = heads((projected[:, :, :width] + b_q).astype(bf16))
    key_rows = heads(projected[:, :, width : 2 * width].astype(bf16))
    values = heads((projected[:, :, 2 * width :] + b_v).astype(bf16))
    scores = jnp.einsum("hqe,hke->hqk", queries, key_rows, preferred_element_type=f32) * score_scale
    row_max = jnp.max(scores, axis=-1, keepdims=True)
    log_total = row_max + jnp.log(jnp.sum(jnp.exp(scores - row_max), axis=-1, keepdims=True))
    attn_probs = jnp.exp(scores - log_total)
    probs_low = attn_probs.astype(bf16)
    attended = unheads(
        jnp.einsum("hqk,hke->hqe", probs_low, values, preferred_element_type=f32).astype(bf16)
    )
    branch_one = jnp.einsum("tre,tde->rd", attended, out_t, preferred_element_type=f32) + b_out_s
    middle = tokens_s + gate_one * branch_one
    normed_two, inv_two = normalize(middle)
    hidden_two = (normed_two * (1.0 + scale_two) + shift_two).astype(bf16)
    pre_act = jnp.einsum("rd,tdf->trf", hidden_two, full_b, preferred_element_type=f32) + b_fc1_t
    activated, gelu_slope = gelu_parts(pre_act)
    act_low = activated.astype(bf16)

    grad_branch_two = (cot * gate_two).astype(bf16)
    grad_b_fc2 = jnp.sum(grad_branch_two.astype(f32), axis=0)
    g_fc2 = scatter(
        lambda a, b: jnp.einsum(
            "rd,trf->tdf", grad_branch_two[:, a:b], act_low, preferred_element_type=f32
        )
    ).T

    branch_two = jnp.einsum("trf,tdf->rd", act_low, full_c, preferred_element_type=f32) + b_fc2_s
    output = restore(middle + gate_two * branch_two)
    grad_gate_two = jnp.sum(cot * branch_two, axis=0)
    grad_pre = (
        jnp.einsum("rd,tdf->trf", grad_branch_two, full_c, preferred_element_type=f32) * gelu_slope
    )
    grad_b_fc1 = jnp.sum(grad_pre, axis=1)
    grad_pre_low = grad_pre.astype(bf16)
    g_fc1 = scatter(
        lambda a, b: jnp.einsum(
            "rd,trf->tdf", hidden_two[:, a:b], grad_pre_low, preferred_element_type=f32
        )
    )
    grad_hidden_two = jnp.einsum("trf,tdf->rd", grad_pre_low, full_b, preferred_element_type=f32)
    grad_shift_two = jnp.sum(grad_hidden_two, axis=0)
    grad_scale_two = jnp.sum(grad_hidden_two * normed_two, axis=0)
    grad_middle = cot + norm_back(grad_hidden_two * (1.0 + scale_two), normed_two, inv_two)
    grad_gate_one = jnp.sum(grad_middle * branch_one, axis=0)
    grad_branch_one = (grad_middle * gate_one).astype(bf16)
    grad_b_out = jnp.sum(grad_branch_one.astype(f32), axis=0)
    grad_attended = heads(
        jnp.einsum("rd,tde->tre", grad_branch_one, out_t, preferred_element_type=f32).astype(bf16)
    )
    grad_values = jnp.einsum("hqk,hqe->hke", probs_low, grad_attended, preferred_element_type=f32)
    grad_probs = jnp.einsum("hqe,hke->hqk", grad_attended, values, preferred_element_type=f32)
    inner_sum = jnp.sum(attn_probs * grad_probs, axis=-1, keepdims=True)
    grad_scores = (attn_probs * (grad_probs - inner_sum) * score_scale).astype(bf16)
    grad_queries = jnp.einsum("hqk,hke->hqe", grad_scores, key_rows, preferred_element_type=f32)
    grad_keys = jnp.einsum("hqk,hqe->hke", grad_scores, queries, preferred_element_type=f32)
    grad_b_q = jnp.sum(grad_queries, axis=1)
    grad_b_v = jnp.sum(grad_values, axis=1)
    grad_proj = jnp.concatenate(
        [unheads(g.astype(bf16)) for g in (grad_queries, grad_keys, grad_values)], axis=2
    )
    g_chunk_a = scatter(
        lambda a, b: jnp.concatenate(
            [
                jnp.einsum("rd,trc->tdc", hidden_one[:, a:b], grad_proj, preferred_element_type=f32),
                jnp.einsum(
                    "rd,tre->tde", grad_branch_one[:, a:b], attended, preferred_element_type=f32
                ),
            ],
            axis=2,
        )
    )
    g_qkv = g_chunk_a[:, : 3 * width].reshape(block, 3, width)
    g_out = g_chunk_a[:, 3 * width :].T
    grad_hidden_one = jnp.einsum("trc,tdc->rd", grad_proj, qkv_t, preferred_element_type=f32)
    grad_shift_one = jnp.sum(grad_hidden_one, axis=0)
    grad_scale_one = jnp.sum(grad_hidden_one * normed_one, axis=0)
    grad_tokens = restore(
        grad_middle + norm_back(grad_hidden_one * (1.0 + scale_one), normed_one, inv_one)
    )

    small = restore(
        jnp.stack(
            [
                grad_shift_one,
                grad_scale_one,
                grad_gate_one,
                grad_shift_two,
                grad_scale_two,
                grad_gate_two,
                grad_b_out,
                grad_b_fc2,
            ]
        )
    )
    biases = jnp.concatenate(
        [
            grad_b_q.reshape(-1),
            grad_b_v.reshape(-1),
            grad_b_fc1.reshape(-1),
            small[6],
            small[7],
        ]
    )
    piece = biases.shape[0] // devices
    mod_send = jnp.broadcast_to(small[:6].reshape(1, n_t, ada_cols), (n_d, n_t, ada_cols))
    first_send = jnp.concatenate(
        [mod_send, biases.reshape(n_d, n_t, piece)], axis=2
    ).reshape(devices, ada_cols + piece)
    first_got = lax.all_to_all(first_send, BOTH, split_axis=0, concat_axis=0, tiled=True)
    grad_mod = first_got[:, :ada_cols]
    bias_piece = jnp.sum(first_got[:, ada_cols:], axis=0)
    gb_ada = jnp.sum(grad_mod, axis=0)
    g_ada = jnp.dot(silu_rows.astype(f32).T, grad_mod, precision=exact)
    silu_part = lax.dot_general(
        grad_mod, w_ada.astype(f32), (((1,), (1,)), ((), ())), precision=exact
    )
    second_send = jnp.concatenate(
        [
            jnp.broadcast_to(silu_part.reshape(n_d, 1, group * block), (n_d, n_t, group * block)),
            jnp.broadcast_to(bias_piece, (n_d, n_t, piece)),
        ],
        axis=2,
    ).reshape(devices, group * block + piece)
    second_got = lax.all_to_all(second_send, BOTH, split_axis=0, concat_axis=0, tiled=True)
    grad_silu = jnp.sum(
        second_got[:, : group * block].reshape(n_d, n_t, group, block), axis=1
    )
    grad_silu = grad_silu.transpose(1, 0, 2).reshape(group, D)
    grad_cond = grad_silu * sig_cond * (1.0 + conditioning * (1.0 - sig_cond))
    summed = second_got[:, group * block :].reshape(-1)
    qv_size = n_t * width
    fc1_own = w_fc1.shape[1]
    fc1_size = n_t * fc1_own
    gb_qv = lax.dynamic_index_in_dim(
        summed[: 2 * qv_size].reshape(2, n_t, width), t_at, 1, keepdims=False
    )
    gb_fc1 = lax.dynamic_index_in_dim(
        summed[2 * qv_size : 2 * qv_size + fc1_size].reshape(n_t, fc1_own), t_at, 0, keepdims=False
    )
    gb_out = summed[2 * qv_size + fc1_size : 2 * qv_size + fc1_size + D]
    gb_fc2 = summed[2 * qv_size + fc1_size + D :]
    return (
        output,
        grad_tokens,
        grad_cond,
        g_ada,
        gb_ada,
        g_qkv,
        gb_qv,
        g_out,
        gb_out,
        g_fc1,
        gb_fc1,
        g_fc2,
        gb_fc2,
    )


def solution(mesh):
    specs = (
        P(("dp", "tensor"), None),
        P("dp", None),
        P(("dp", "tensor"), None),
        P("dp", "tensor"),
        P("tensor"),
        P("dp", None, "tensor"),
        P(None, "tensor"),
        P("tensor", "dp"),
        P(),
        P("dp", "tensor"),
        P("tensor"),
        P("tensor", "dp"),
        P(),
    )
    out_specs = (specs[0], specs[0], specs[1]) + specs[3:]
    return jax.shard_map(body, mesh=mesh, in_specs=specs, out_specs=out_specs, check_vma=False)
```

```python
import jax
import jax.numpy as jnp
from jax import lax
from jax.experimental import pallas as pl
from jax.experimental.pallas import tpu as pltpu
from jax.sharding import PartitionSpec as P

D = 768
HD = 64
SEQ = 256


epsilon = 1e-06
gelu_coef = 0.7978845608028654
cube_coef = 0.044715
f32 = jnp.float32
bf16 = jnp.bfloat16
BOTH = ("dp", "tensor")


def gelu_parts(pre_act):
    inner_arg = gelu_coef * (pre_act + cube_coef * pre_act * pre_act * pre_act)
    tangent = jnp.tanh(inner_arg)
    result = 0.5 * pre_act * (1.0 + tangent)
    gelu_slope = 0.5 * (1.0 + tangent) + 0.5 * pre_act * (1.0 - tangent * tangent) * gelu_coef * (
        1.0 + 3.0 * cube_coef * pre_act * pre_act
    )
    return (result, gelu_slope)


def normalize(rows_in):
    center = rows_in - jnp.mean(rows_in, axis=-1, keepdims=True)
    inv_std = lax.rsqrt(jnp.mean(center * center, axis=-1, keepdims=True) + epsilon)
    return (center * inv_std, inv_std)


def norm_back(grad_normed, normed, inv_std):
    return inv_std * (
        grad_normed
        - jnp.mean(grad_normed, axis=-1, keepdims=True)
        - normed * jnp.mean(grad_normed * normed, axis=-1, keepdims=True)
    )


def barrier(*values):
    return lax.optimization_barrier(values)


def swap_dp(value, bit):
    size = lax.axis_size("dp")
    return lax.ppermute(value, "dp", [(i, i ^ bit) for i in range(size)])


def swap_tensor(value, bit):
    size = lax.axis_size("tensor")
    return lax.ppermute(value, "tensor", [(i, i ^ bit) for i in range(size)])


HALF = D // 2


def feature_order(block):
    me = lax.axis_index("dp")
    place = lax.broadcasted_iota(jnp.int32, (D, D), 1)
    source = lax.broadcasted_iota(jnp.int32, (D, D), 0)
    slot = place // block
    flip = ((slot // 2) % 2) * 4 + (slot % 2) * 2 + slot // 4
    return ((me ^ flip) * block + place % block == source).astype(f32)


def by_slot(value):
    me = lax.axis_index("tensor")
    return jnp.stack(
        [lax.dynamic_index_in_dim(value, me ^ j, 0, keepdims=False) for j in range(4)]
    )


VM = pl.BlockSpec(memory_space=pltpu.VMEM)
ANY = pl.BlockSpec(memory_space=pl.ANY)


def shaped(shape, kind):
    return jax.ShapeDtypeStruct(shape, kind)


def run(kernel, name, operands, pieces, outs, scratch=(), flops=0):
    n_sem = 4 * max(len(p) // 2, 1) if (p := pieces[0] if pieces else ()) else 0
    flat = [ref for group in pieces for ref in group]
    loads = [pltpu.VMEM((4, D, D), bf16) for _ in pieces]
    sems = [pltpu.SemaphoreType.DMA((n_sem,)) for _ in pieces]
    moved = sum(v.size * v.dtype.itemsize for v in list(operands) + flat)
    moved += sum(int(o.size) * o.dtype.itemsize for o in outs)

    def wrapped(*refs):
        n_in, n_flat, n_out = len(operands), len(flat), len(outs)
        ins = refs[:n_in]
        raw = refs[n_in : n_in + n_flat]
        out_refs = refs[n_in + n_flat : n_in + n_flat + n_out]
        rest = refs[n_in + n_flat + n_out :]
        chunks, at = [], 0
        for which, group in enumerate(pieces):
            chunks.append(
                start_load(raw[at : at + len(group)], rest[which], rest[len(pieces) + which])
            )
            at += len(group)
        kernel(*ins, *chunks, *out_refs, *rest[2 * len(pieces) :])

    return pl.pallas_call(
        wrapped,
        name=name,
        out_shape=tuple(outs),
        in_specs=[VM] * len(operands) + [ANY] * len(flat),
        out_specs=tuple([VM] * len(outs)),
        scratch_shapes=loads + sems + list(scratch),
        cost_estimate=pl.CostEstimate(flops=flops, bytes_accessed=moved, transcendentals=0),
    )(*operands, *flat)


def start_load(refs, full, sems):
    copies = []
    for j in range(4):
        if len(refs) == 1:
            slot = [pltpu.make_async_copy(refs[0].at[j], full.at[j], sems.at[j])]
        else:
            slot = []
            for p in range(8):
                c, yx = p // 4, p % 4
                source = refs[((j // 2) * 4 + yx) * 2 + c]
                block = source.shape[1]
                slot.append(
                    pltpu.make_async_copy(
                        source.at[j % 2], full.at[j, pl.ds(p * block, block)], sems.at[j * 8 + p]
                    )
                )
        for copy in slot:
            copy.start()
        copies.append(slot)

    def get(j):
        for copy in copies[j]:
            copy.wait()
        return full[j]

    return get


def dot(a, b):
    return jnp.dot(a, b, preferred_element_type=f32)


def dot_nt(a, b):
    return lax.dot_general(a, b, (((1,), (1,)), ((), ())), preferred_element_type=f32)


def turned(value):
    return value.astype(f32).T.astype(bf16)


def total(value):
    return jnp.sum(value, axis=0, keepdims=True)


def soft(q, k):
    scores = dot_nt(q, k) * (HD ** (-0.5))
    row_max = jnp.max(scores, axis=-1, keepdims=True)
    log_total = row_max + jnp.log(jnp.sum(jnp.exp(scores - row_max), axis=-1, keepdims=True))
    return jnp.exp(scores - log_total)


def attention_forward(tokens, mods, bias, chunk, hidden, proj, att, branch, middle, hidden_two):
    normed, _ = normalize(tokens[...])
    hidden[...] = (normed * (1.0 + mods[1:2]) + mods[0:1]).astype(bf16)
    width = att.shape[2]
    acc = None
    for j in range(4):
        weight = chunk(j)
        proj[j] = (dot(hidden[...], weight) + bias[j]).astype(bf16)
        for h in range(width // HD):
            q = proj[j, :, h * HD : h * HD + HD]
            k = proj[j, :, width + h * HD : width + h * HD + HD]
            v = proj[j, :, 2 * width + h * HD : 2 * width + h * HD + HD]
            att[j, :, h * HD : h * HD + HD] = dot(soft(q, k).astype(bf16), v).astype(bf16)
        term = dot_nt(att[j], weight[:, 3 * width :])
        acc = term if acc is None else acc + term
    branch_one = acc + mods[6:7]
    branch[...] = branch_one
    middle_now = tokens[...] + mods[2:3] * branch_one
    middle[...] = middle_now
    normed_two, _ = normalize(middle_now)
    hidden_two[...] = (normed_two * (1.0 + mods[4:5]) + mods[3:4]).astype(bf16)


def hidden_units(hidden_two, cot, mods, bias, chunk, act, slope, grad_two, away, mine):
    grad_two[...] = (cot[...] * mods[5:6]).astype(bf16)
    grad_turned = turned(grad_two[...])
    for j in range(4):
        pre = dot(hidden_two[...], chunk(j)) + bias[j]
        value, slope_now = gelu_parts(pre)
        act[j] = value.astype(bf16)
        slope[j] = slope_now
        away[j] = dot(grad_turned[HALF:], act[j]).astype(bf16)
        mine[j] = dot(grad_turned[:HALF], act[j])


def hidden_back(hidden_two, grad_two, slope, chunk, grad_pre, sums, away, mine):
    hidden_turned = turned(hidden_two[...])
    for j in range(4):
        grad = dot(grad_two[...], chunk(j)) * slope[j]
        sums[j] = total(grad)
        grad_pre[j] = grad.astype(bf16)
        away[j] = dot(hidden_turned[HALF:], grad_pre[j]).astype(bf16)
        mine[j] = dot(hidden_turned[:HALF], grad_pre[j])


def middle_back(
    act, grad_pre, cot, middle, branch_one, grad_two, mods, chunk_c, chunk_b,
    out, grad_middle, grad_one, rows,
):
    back = None
    branch_two = None
    for j in range(4):
        term = dot_nt(act[j], chunk_c(j))
        branch_two = term if branch_two is None else branch_two + term
        term = dot_nt(grad_pre[j], chunk_b(j))
        back = term if back is None else back + term
    branch_two = branch_two + mods[7:8]
    out[...] = middle[...] + mods[5:6] * branch_two
    rows[...] = jnp.zeros_like(rows)
    rows[5:6] = total(cot[...] * branch_two)
    normed, inv = normalize(middle[...])
    rows[3:4] = total(back)
    rows[4:5] = total(back * normed)
    grad = cot[...] + norm_back(back * (1.0 + mods[4:5]), normed, inv)
    grad_middle[...] = grad
    rows[2:3] = total(grad * branch_one[...])
    grad_one[...] = (grad * mods[2:3]).astype(bf16)
    rows[6:7] = total(grad_one[...].astype(f32))
    rows[7:8] = total(grad_two[...].astype(f32))


def attention_back(grad_one, proj, att, hidden, chunk, away, mine, sums, back, wide):
    hidden_turned = turned(hidden[...])
    grad_turned = turned(grad_one[...])
    width = att.shape[2]
    wide[...] = jnp.zeros_like(wide)
    acc = None
    for j in range(4):
        weight = chunk(j)
        grad_att = dot(grad_one[...], weight[:, 3 * width :]).astype(bf16)
        for h in range(width // HD):
            lo, hi = h * HD, h * HD + HD
            q = proj[j, :, lo:hi]
            k = proj[j, :, width + lo : width + hi]
            v = proj[j, :, 2 * width + lo : 2 * width + hi]
            probs = soft(q, k)
            g = grad_att[:, lo:hi]
            wide[:, 2 * width + lo : 2 * width + hi] = dot(turned(probs.astype(bf16)), g)
            grad_probs = dot_nt(g, v)
            inner = jnp.sum(probs * grad_probs, axis=-1, keepdims=True)
            scores = (probs * (grad_probs - inner) * (HD ** (-0.5))).astype(bf16)
            wide[:, lo:hi] = dot(scores, k)
            wide[:, width + lo : width + hi] = dot(turned(scores), q)
        sums[j] = total(wide[...])
        grad_proj = wide[...].astype(bf16)
        away[j] = dot(hidden_turned[HALF:], grad_proj).astype(bf16)
        away[j, :, 3 * width :] = dot(grad_turned[HALF:], att[j]).astype(bf16)
        mine[j] = dot(hidden_turned[:HALF], grad_proj)
        mine[j, :, 3 * width :] = dot(grad_turned[:HALF], att[j])
        term = dot_nt(grad_proj, weight)
        acc = term if acc is None else acc + term
    back[...] = acc


def token_back(tokens, grad_middle, back, mods, grad_tokens, rows):
    normed, inv = normalize(tokens[...])
    rows[...] = jnp.zeros_like(rows)
    rows[0:1] = total(back[...])
    rows[1:2] = total(back[...] * normed)
    grad_tokens[...] = grad_middle[...] + norm_back(back[...] * (1.0 + mods[1:2]), normed, inv)


def pack_pairs(first, second, third, fourth, low, high):
    low[0] = first[...]
    low[1] = second[...]
    high[0] = third[...]
    high[1] = fourth[...]


def add_first(mine, got, send_low, send_high, keep_low, keep_high):
    block = keep_low.shape[2]

    def rows(j, y, x):
        at = pl.ds((2 * y + x) * block, block)
        return mine[j, at] + got[j, at].astype(f32)

    for j in range(2):
        for k in range(2):
            keep_low[j, k] = rows(j, k, 0)
            send_low[j, k] = rows(j, k, 1).astype(bf16)
            keep_high[j, k] = rows(2 + j, 0, k)
            send_high[j, k] = rows(2 + j, 1, k).astype(bf16)


def add_second(keep_low, keep_high, low, high, send_low, send_high, keep):
    for j in range(2):
        send_low[j] = (keep_low[j, 1] + low[j, 1].astype(f32)).astype(bf16)
        send_high[j] = (keep_high[j, 1] + high[j, 1].astype(f32)).astype(bf16)
        keep[j] = keep_low[j, 0] + low[j, 0].astype(f32)
        keep[2 + j] = keep_high[j, 0] + high[j, 0].astype(f32)


def add_third(keep, low, high, own, one, two, three):
    own[...] = keep[0] + low[0].astype(f32)
    one[...] = (keep[1] + low[1].astype(f32)).astype(bf16)
    two[...] = (keep[2] + high[0].astype(f32)).astype(bf16)
    three[...] = (keep[3] + high[1].astype(f32)).astype(bf16)


def gather_custom(chunk_a, chunk_b, chunk_c):
    block = chunk_a.shape[0]
    pair = shaped((2, block, D), bf16)

    def along(chunk):
        return [chunk] + [swap_tensor(chunk, j) for j in (1, 2, 3)]

    def first(blocks):
        low, high = run(pack_pairs, "pack", blocks, (), (pair, pair))
        return [low, high, swap_dp(low, 2), swap_dp(high, 4), swap_dp(low, 4), swap_dp(high, 2)]

    def second(got):
        low, high, low_x, high_y, low_y, high_x = got
        return [low, low_x, low_y, swap_dp(low_x, 4), high, high_x, high_y, swap_dp(high_y, 2)]

    def third(held):
        return [piece for part in held for piece in (part, swap_dp(part, 1))]

    za = along(chunk_a)
    za, chunk_b = barrier(za, chunk_b)
    zb = along(chunk_b)
    one_a = first(za)
    zb, one_a, chunk_c = barrier(zb, one_a, chunk_c)
    zc = along(chunk_c)
    two_a = second(one_a)
    one_b = first(zb)
    zc, two_a, one_b = barrier(zc, two_a, one_b)
    three_a = third(two_a)
    two_b = second(one_b)
    one_c = first(zc)
    two_b, one_c = barrier(two_b, one_c)
    three_b = third(two_b)
    two_c = second(one_c)
    return three_a, three_b, third(two_c)


def scatter_custom(away, mine):
    block = mine.shape[1] // 4
    pair = shaped((2, block, D), bf16)
    wide = shaped((2, 2, block, D), bf16)
    got = swap_dp(away, 1)
    send_low, send_high, keep_low, keep_high = run(
        add_first,
        "add_first",
        (mine, got),
        (),
        (wide, wide, shaped(wide.shape, f32), shaped(wide.shape, f32)),
    )
    low, high = swap_dp(send_low, 2), swap_dp(send_high, 4)
    send_low, send_high, keep = run(
        add_second,
        "add_second",
        (keep_low, keep_high, low, high),
        (),
        (pair, pair, shaped((4, block, D), f32)),
    )
    low, high = swap_dp(send_low, 4), swap_dp(send_high, 2)
    one = shaped((block, D), bf16)
    own, *sends = run(
        add_third, "add_third", (keep, low, high), (), (shaped((block, D), f32), one, one, one)
    )
    for j in (1, 2, 3):
        own = own + swap_tensor(sends[j - 1], j).astype(f32)
    return own


def gather_plain(*chunks):
    full = []
    for chunk in chunks:
        near = by_slot(lax.all_gather(chunk, "tensor", axis=0))
        full.append([lax.all_gather(near, "dp", axis=1, tiled=True)])
    return full


def scatter_plain(away, mine):
    grad = by_slot(jnp.concatenate([mine, away.astype(f32)], axis=1))
    near = lax.psum_scatter(grad, "tensor", scatter_dimension=0, tiled=True)[0]
    return lax.psum_scatter(near, "dp", scatter_dimension=0, tiled=True)


def body(
    tokens,
    conditioning,
    cotangent,
    w_ada,
    b_ada,
    w_qkv,
    b_qv,
    w_out,
    b_out,
    w_fc1,
    b_fc1,
    w_fc2,
    b_fc2,
):
    n_d = lax.axis_size("dp")
    n_t = lax.axis_size("tensor")
    devices = n_d * n_t
    dp_at = lax.axis_index("dp")
    t_at = lax.axis_index("tensor")
    custom = n_d == 8 and n_t == 4
    block = w_fc1.shape[0]
    width = w_qkv.shape[2]
    ada_cols = w_ada.shape[1]
    group = conditioning.shape[0]
    exact = lax.Precision.HIGHEST

    if custom:
        order = feature_order(block)
        shuffle = lambda v: jnp.dot(v, order, precision=exact)
        restore = lambda v: lax.dot_general(v, order, (((1,), (1,)), ((), ())), precision=exact)
        gather, scatter = gather_custom, scatter_custom
    else:
        shuffle = restore = lambda v: v
        gather, scatter = gather_plain, scatter_plain

    chunk_a = jnp.concatenate([w_qkv.reshape(block, 3 * width), w_out.T], axis=1)
    full_a, full_b, full_c = gather(chunk_a, w_fc1, w_fc2.T)

    sig_cond = jax.nn.sigmoid(conditioning)
    silu_cond = (conditioning * sig_cond).astype(bf16)
    silu_send = silu_cond.reshape(group, n_d, block).transpose(1, 0, 2)
    silu_rows = lax.all_to_all(silu_send, "dp", split_axis=0, concat_axis=0, tiled=True)
    silu_rows = silu_rows.reshape(n_d * group, block)
    mod_part = jnp.dot(silu_rows, w_ada, preferred_element_type=f32)
    mod_part = mod_part + (dp_at == 0).astype(f32) * b_ada
    bias_own = jnp.concatenate([b_qv.reshape(-1), b_fc1])
    head_send = jnp.concatenate(
        [mod_part, jnp.broadcast_to(bias_own, (devices, bias_own.shape[0]))], axis=1
    )
    head_got = lax.all_to_all(head_send, BOTH, split_axis=0, concat_axis=0, tiled=True)
    head_got = head_got.reshape(n_d, n_t, head_send.shape[1])
    modulation = jnp.sum(head_got[:, :, :ada_cols], axis=0).reshape(6, D)
    mods = shuffle(jnp.concatenate([modulation, b_out[None], b_fc2[None]], axis=0))
    bias_all = by_slot(head_got[0, :, ada_cols:])
    none = jnp.zeros((n_t, width), f32)
    bias_a = jnp.concatenate(
        [bias_all[:, :width], none, bias_all[:, width : 2 * width], none], axis=1
    )[:, None]
    bias_b = bias_all[:, None, 2 * width :]

    tokens_s = shuffle(tokens)
    cot = shuffle(cotangent)
    rows_f = shaped((SEQ, D), f32)
    rows_b = shaped((SEQ, D), bf16)
    slots_b = shaped((n_t, SEQ, D), bf16)
    sums_f = shaped((n_t, 1, D), f32)
    away_b = shaped((n_t, HALF, D), bf16)
    mine_f = shaped((n_t, HALF, D), f32)
    vectors = shaped((8, D), f32)
    unit = 2 * SEQ * D * D * n_t
    hidden_one, proj, attended, branch_one, middle, hidden_two = run(
        attention_forward,
        "attention_forward",
        (tokens_s, mods, bias_a),
        (full_a,),
        (rows_b, slots_b, shaped((n_t, SEQ, width), bf16), rows_f, rows_f, rows_b),
        flops=2 * unit,
    )
    act, slope, grad_two, away_c, mine_c = run(
        hidden_units,
        "hidden_units",
        (hidden_two, cot, mods, bias_b),
        (full_b,),
        (slots_b, shaped(slots_b.shape, f32), rows_b, away_b, mine_f),
        flops=2 * unit,
    )
    g_fc2 = scatter(away_c, mine_c).T
    grad_pre, sums_b, away_b1, mine_b1 = run(
        hidden_back,
        "hidden_back",
        (hidden_two, grad_two, slope),
        (full_c,),
        (slots_b, sums_f, away_b, mine_f),
        flops=2 * unit,
    )
    g_fc1 = scatter(away_b1, mine_b1)
    output, grad_middle, grad_one, rows_mid = run(
        middle_back,
        "middle_back",
        (act, grad_pre, cot, middle, branch_one, grad_two, mods),
        (full_c, full_b),
        (rows_f, rows_f, rows_b, vectors),
        flops=2 * unit,
    )
    output = restore(output)
    away_a, mine_a, sums_a, back = run(
        attention_back,
        "attention_back",
        (grad_one, proj, attended, hidden_one),
        (full_a,),
        (away_b, mine_f, sums_f, rows_f),
        scratch=[pltpu.VMEM((SEQ, D), f32)],
        flops=3 * unit,
    )
    g_chunk_a = scatter(away_a, mine_a)
    g_qkv = g_chunk_a[:, : 3 * width].reshape(block, 3, width)
    g_out = g_chunk_a[:, 3 * width :].T
    grad_tokens, rows_top = run(
        token_back,
        "token_back",
        (tokens_s, grad_middle, back, mods),
        (),
        (rows_f, vectors),
    )
    grad_tokens = restore(grad_tokens)

    small = restore(rows_mid + rows_top)
    sums_a = by_slot(sums_a[:, 0])
    biases = jnp.concatenate(
        [
            sums_a[:, :width].reshape(-1),
            sums_a[:, 2 * width : 3 * width].reshape(-1),
            by_slot(sums_b[:, 0]).reshape(-1),
            small[6],
            small[7],
        ]
    )
    piece = biases.shape[0] // devices
    mod_send = jnp.broadcast_to(small[:6].reshape(1, n_t, ada_cols), (n_d, n_t, ada_cols))
    first_send = jnp.concatenate(
        [mod_send, biases.reshape(n_d, n_t, piece)], axis=2
    ).reshape(devices, ada_cols + piece)
    first_got = lax.all_to_all(first_send, BOTH, split_axis=0, concat_axis=0, tiled=True)
    grad_mod = first_got[:, :ada_cols]
    bias_piece = jnp.sum(first_got[:, ada_cols:], axis=0)
    gb_ada = jnp.sum(grad_mod, axis=0)
    g_ada = jnp.dot(silu_rows.astype(f32).T, grad_mod, precision=exact)
    silu_part = lax.dot_general(
        grad_mod, w_ada.astype(f32), (((1,), (1,)), ((), ())), precision=exact
    )
    second_send = jnp.concatenate(
        [
            jnp.broadcast_to(silu_part.reshape(n_d, 1, group * block), (n_d, n_t, group * block)),
            jnp.broadcast_to(bias_piece, (n_d, n_t, piece)),
        ],
        axis=2,
    ).reshape(devices, group * block + piece)
    second_got = lax.all_to_all(second_send, BOTH, split_axis=0, concat_axis=0, tiled=True)
    grad_silu = jnp.sum(
        second_got[:, : group * block].reshape(n_d, n_t, group, block), axis=1
    )
    grad_silu = grad_silu.transpose(1, 0, 2).reshape(group, D)
    grad_cond = grad_silu * sig_cond * (1.0 + conditioning * (1.0 - sig_cond))
    summed = second_got[:, group * block :].reshape(-1)
    qv_size = n_t * width
    fc1_own = w_fc1.shape[1]
    fc1_size = n_t * fc1_own
    gb_qv = lax.dynamic_index_in_dim(
        summed[: 2 * qv_size].reshape(2, n_t, width), t_at, 1, keepdims=False
    )
    gb_fc1 = lax.dynamic_index_in_dim(
        summed[2 * qv_size : 2 * qv_size + fc1_size].reshape(n_t, fc1_own), t_at, 0, keepdims=False
    )
    gb_out = summed[2 * qv_size + fc1_size : 2 * qv_size + fc1_size + D]
    gb_fc2 = summed[2 * qv_size + fc1_size + D :]
    return (
        output,
        grad_tokens,
        grad_cond,
        g_ada,
        gb_ada,
        g_qkv,
        gb_qv,
        g_out,
        gb_out,
        g_fc1,
        gb_fc1,
        g_fc2,
        gb_fc2,
    )


def solution(mesh):
    specs = (
        P(("dp", "tensor"), None),
        P("dp", None),
        P(("dp", "tensor"), None),
        P("dp", "tensor"),
        P("tensor"),
        P("dp", None, "tensor"),
        P(None, "tensor"),
        P("tensor", "dp"),
        P(),
        P("dp", "tensor"),
        P("tensor"),
        P("tensor", "dp"),
        P(),
    )
    out_specs = (specs[0], specs[0], specs[1]) + specs[3:]
    return jax.shard_map(body, mesh=mesh, in_specs=specs, out_specs=out_specs, check_vma=False)
```

```python
import jax
import jax.numpy as jnp
from jax import lax
from jax.experimental import pallas as pl
from jax.experimental.pallas import tpu as pltpu
from jax.sharding import PartitionSpec as P


D = 768
HD = 64
SEQ = 256


epsilon = 1e-06
gelu_coef = 0.7978845608028654
cube_coef = 0.044715
f32 = jnp.float32
bf16 = jnp.bfloat16
BOTH = ("dp", "tensor")


def gelu_parts(pre_act):
    inner_arg = gelu_coef * (pre_act + cube_coef * pre_act * pre_act * pre_act)
    tangent = jnp.tanh(inner_arg)
    result = 0.5 * pre_act * (1.0 + tangent)
    gelu_slope = 0.5 * (1.0 + tangent) + 0.5 * pre_act * (1.0 - tangent * tangent) * gelu_coef * (
        1.0 + 3.0 * cube_coef * pre_act * pre_act
    )
    return (result, gelu_slope)


def normalize(rows_in):
    center = rows_in - jnp.mean(rows_in, axis=-1, keepdims=True)
    inv_std = lax.rsqrt(jnp.mean(center * center, axis=-1, keepdims=True) + epsilon)
    return (center * inv_std, inv_std)


def norm_back(grad_normed, normed, inv_std):
    return inv_std * (
        grad_normed
        - jnp.mean(grad_normed, axis=-1, keepdims=True)
        - normed * jnp.mean(grad_normed * normed, axis=-1, keepdims=True)
    )


def barrier(*values):
    return lax.optimization_barrier(values)


def swap_dp(value, bit):
    size = lax.axis_size("dp")
    return lax.ppermute(value, "dp", [(i, i ^ bit) for i in range(size)])


def swap_tensor(value, bit):
    size = lax.axis_size("tensor")
    return lax.ppermute(value, "tensor", [(i, i ^ bit) for i in range(size)])


HALF = D // 2


def feature_order(block):
    me = lax.axis_index("dp")
    place = lax.broadcasted_iota(jnp.int32, (D, D), 1)
    source = lax.broadcasted_iota(jnp.int32, (D, D), 0)
    slot = place // block
    flip = ((slot // 2) % 2) * 4 + (slot % 2) * 2 + slot // 4
    return ((me ^ flip) * block + place % block == source).astype(f32)


def by_slot(value):
    me = lax.axis_index("tensor")
    return jnp.stack(
        [lax.dynamic_index_in_dim(value, me ^ j, 0, keepdims=False) for j in range(4)]
    )


VM = pl.BlockSpec(memory_space=pltpu.VMEM)
ANY = pl.BlockSpec(memory_space=pl.ANY)


def shaped(shape, kind):
    return jax.ShapeDtypeStruct(shape, kind)


def spec_of(shape):
    if len(shape) == 3 and shape[0] == 4:
        return pl.BlockSpec((None,) + tuple(shape[1:]), lambda j: (j, 0, 0))
    return pl.BlockSpec(tuple(shape), lambda j: (0,) * len(shape))


def run(kernel, operands, pieces, outs, scratch=(), flops=0):
    flat = [ref for group in pieces for ref in group]
    loads = [pltpu.VMEM((4, D, D), bf16) for _ in pieces]
    sems = [pltpu.SemaphoreType.DMA((4 * max(len(group) // 2, 1),)) for group in pieces]
    moved = sum(v.size * v.dtype.itemsize for v in list(operands) + flat)
    moved += sum(int(o.size) * o.dtype.itemsize for o in outs)

    def wrapped(*refs):
        n_in, n_flat, n_out = len(operands), len(flat), len(outs)
        ins = refs[:n_in]
        raw = refs[n_in : n_in + n_flat]
        out_refs = refs[n_in + n_flat : n_in + n_flat + n_out]
        rest = refs[n_in + n_flat + n_out :]
        chunks, at = [], 0
        for which, group in enumerate(pieces):
            chunks.append(
                start_load(raw[at : at + len(group)], rest[which], rest[len(pieces) + which])
            )
            at += len(group)
        kernel(*ins, *chunks, *out_refs, *rest[2 * len(pieces) :])

    return pl.pallas_call(
        wrapped,
        grid=(4,),
        out_shape=tuple(outs),
        in_specs=[spec_of(v.shape) for v in operands] + [ANY] * len(flat),
        out_specs=tuple(spec_of(o.shape) for o in outs),
        scratch_shapes=loads + sems + list(scratch),
        cost_estimate=pl.CostEstimate(flops=flops, bytes_accessed=moved, transcendentals=0),
    )(*operands, *flat)


def run_blocks(kernel, grid, operands, outs, flops=0):
    moved = sum(v.size * v.dtype.itemsize for v, _ in operands)
    moved += sum(int(o.size) * o.dtype.itemsize for o, _ in outs)
    return pl.pallas_call(
        kernel,
        grid=grid,
        out_shape=tuple(o for o, _ in outs),
        in_specs=[spec for _, spec in operands],
        out_specs=tuple(spec for _, spec in outs),
        cost_estimate=pl.CostEstimate(flops=flops, bytes_accessed=moved, transcendentals=0),
    )(*[v for v, _ in operands])


def start_load(refs, full, sems):
    step = pl.program_id(0)
    count = 1 if len(refs) == 1 else 8
    size = D // count

    @pl.when(step == 0)
    def _():
        for j in range(4):
            if count == 1:
                pltpu.make_async_copy(refs[0].at[j], full.at[j], sems.at[j]).start()
                continue
            for p in range(8):
                source = refs[((j // 2) * 4 + p % 4) * 2 + p // 4]
                pltpu.make_async_copy(
                    source.at[j % 2], full.at[j, pl.ds(p * size, size)], sems.at[j * 8 + p]
                ).start()

    def get():
        for p in range(count):
            pltpu.make_async_copy(
                refs[0].at[0], full.at[step, pl.ds(p * size, size)], sems.at[step * count + p]
            ).wait()
        return full[step]

    return get


def opening(act):
    pl.when(pl.program_id(0) == 0)(act)


def closing(act):
    pl.when(pl.program_id(0) == 3)(act)


def dot(a, b):
    return jnp.dot(a, b, preferred_element_type=f32)


def dot_nt(a, b):
    return lax.dot_general(a, b, (((1,), (1,)), ((), ())), preferred_element_type=f32)


def turned(value):
    return value.astype(f32).T.astype(bf16)


def total(value):
    return jnp.sum(value, axis=0, keepdims=True)


def soft(q, k):
    scores = dot_nt(k, q) * (HD ** (-0.5))
    top = jnp.max(scores, axis=0, keepdims=True)
    log_total = top + jnp.log(jnp.sum(jnp.exp(scores - top), axis=0, keepdims=True))
    return jnp.exp(scores - log_total)


def attention_forward(tokens, mods, bias, chunk, hidden, proj, att, branch, middle, hidden_two):
    @opening
    def _():
        normed, _ = normalize(tokens[...])
        hidden[...] = (normed * (1.0 + mods[1:2]) + mods[0:1]).astype(bf16)
        branch[...] = jnp.broadcast_to(mods[6:7], branch.shape)

    width = att.shape[1]
    weight = chunk()
    now = (dot(hidden[...], weight) + bias[...]).astype(bf16)
    proj[...] = now
    values = turned(now[:, 2 * width : 3 * width])
    heads = []
    for lo in range(0, width, HD):
        probs = soft(now[:, lo : lo + HD], now[:, width + lo : width + lo + HD])
        heads.append(dot(values[lo : lo + HD], probs.astype(bf16)))
    att[...] = jnp.concatenate(heads, axis=0).T.astype(bf16)
    branch[...] += dot_nt(att[...], weight[:, 3 * width :])

    @closing
    def _():
        middle_now = tokens[...] + mods[2:3] * branch[...]
        middle[...] = middle_now
        normed_two, _ = normalize(middle_now)
        hidden_two[...] = (normed_two * (1.0 + mods[4:5]) + mods[3:4]).astype(bf16)


def hidden_units(
    hidden_two, cot, mods, bias, chunk, act, slope, grad_two, away, grad_turned
):
    @opening
    def _():
        grad_two[...] = (cot[...] * mods[5:6]).astype(bf16)
        grad_turned[...] = turned(grad_two[...])

    value, slope_now = gelu_parts(dot(hidden_two[...], chunk()) + bias[...])
    low = value.astype(bf16)
    act[...] = low
    slope[...] = slope_now
    away[...] = dot(grad_turned[HALF:], low).astype(bf16)


def hidden_back(hidden_two, grad_two, slope, chunk, grad_pre, sums, away, hidden_turned):
    @opening
    def _():
        hidden_turned[...] = turned(hidden_two[...])

    grad = dot(grad_two[...], chunk()) * slope[...]
    sums[...] = total(grad)
    low = grad.astype(bf16)
    grad_pre[...] = low
    away[...] = dot(hidden_turned[HALF:], low).astype(bf16)


def middle_back(
    act, grad_pre, cot, middle, branch_one, grad_two, mods, chunk_c, chunk_b,
    out, grad_middle, grad_one, rows, two, back,
):
    @opening
    def _():
        two[...] = jnp.broadcast_to(mods[7:8], two.shape)
        back[...] = jnp.zeros_like(back)

    two[...] += dot_nt(act[...], chunk_c())
    back[...] += dot_nt(grad_pre[...], chunk_b())

    @closing
    def _():
        branch_two = two[...]
        grad_hidden = back[...]
        out[...] = middle[...] + mods[5:6] * branch_two
        normed, inv = normalize(middle[...])
        grad = cot[...] + norm_back(grad_hidden * (1.0 + mods[4:5]), normed, inv)
        grad_middle[...] = grad
        grad_one[...] = (grad * mods[2:3]).astype(bf16)
        rows[0:2] = jnp.zeros_like(rows[0:2])
        rows[2:3] = total(grad * branch_one[...])
        rows[3:4] = total(grad_hidden)
        rows[4:5] = total(grad_hidden * normed)
        rows[5:6] = total(cot[...] * branch_two)
        rows[6:7] = total(grad_one[...].astype(f32))
        rows[7:8] = total(grad_two[...].astype(f32))


def attention_back(
    grad_one, proj, att, hidden, chunk, away, grads, sums, back, hidden_turned, grad_turned, wide
):
    @opening
    def _():
        wide[...] = jnp.zeros_like(wide)
        back[...] = jnp.zeros_like(back)
        hidden_turned[...] = turned(hidden[...])
        grad_turned[...] = turned(grad_one[...])

    width = att.shape[1]
    weight = chunk()
    now = proj[...]
    grad_att = dot(grad_one[...], weight[:, 3 * width :]).astype(bf16)
    keys = turned(now[:, width : 2 * width])
    query_grads = []
    for lo in range(0, width, HD):
        hi = lo + HD
        q = now[:, lo:hi]
        g = grad_att[:, lo:hi]
        probs = soft(q, now[:, width + lo : width + hi])
        wide[:, 2 * width + lo : 2 * width + hi] = dot(probs.astype(bf16), g)
        grad_probs = dot_nt(now[:, 2 * width + lo : 2 * width + hi], g)
        inner = jnp.sum(probs * grad_probs, axis=0, keepdims=True)
        scores = (probs * (grad_probs - inner) * (HD ** (-0.5))).astype(bf16)
        query_grads.append(dot(keys[lo:hi], scores))
        wide[:, width + lo : width + hi] = dot(scores, q)
    wide[:, :width] = jnp.concatenate(query_grads, axis=0).T
    sums[...] = total(wide[...])
    grad_proj = wide[...].astype(bf16)
    grads[...] = grad_proj
    away[...] = dot(hidden_turned[HALF:], grad_proj).astype(bf16)
    away[:, 3 * width :] = dot(grad_turned[HALF:], att[...]).astype(bf16)
    back[...] += dot_nt(grad_proj, weight)


def token_back(tokens, grad_middle, back, mods, grad_tokens, rows):
    @opening
    def _():
        normed, inv = normalize(tokens[...])
        rows[...] = jnp.zeros_like(rows)
        rows[0:1] = total(back[...])
        rows[1:2] = total(back[...] * normed)
        grad_tokens[...] = grad_middle[...] + norm_back(
            back[...] * (1.0 + mods[1:2]), normed, inv
        )


def pack_pairs(first, second, third, fourth, low, high):
    low[0] = first[...]
    low[1] = second[...]
    high[0] = third[...]
    high[1] = fourth[...]


def add_first(*refs):
    *ins, send_low, send_high, keep_low, keep_high = refs
    turn, low, high, low_got, high_got = ins[:5]
    low_now = dot(turn[...], low[...])
    high_now = dot(turn[...], high[...])
    if len(ins) > 5:
        turn_two, low_two, high_two = ins[5:]
        cut = D - low_two.shape[1]
        low_now = jnp.concatenate([low_now[:, :cut], dot(turn_two[...], low_two[...])], axis=1)
        high_now = jnp.concatenate([high_now[:, :cut], dot(turn_two[...], high_two[...])], axis=1)
    low_now = low_now + low_got[...].astype(f32)
    high_now = high_now + high_got[...].astype(f32)
    block = keep_low.shape[1]
    for k in range(2):
        at = 2 * k * block
        keep_low[k] = low_now[at : at + block]
        send_low[k] = low_now[at + block : at + 2 * block].astype(bf16)
        at = k * block
        keep_high[k] = high_now[at : at + block]
        send_high[k] = high_now[at + 2 * block : at + 3 * block].astype(bf16)


def add_second(keep_low, keep_high, low, high, send_low, send_high, keep):
    send_low[...] = (keep_low[1] + low[1].astype(f32)).astype(bf16)
    send_high[...] = (keep_high[1] + high[1].astype(f32)).astype(bf16)
    keep[0] = keep_low[0] + low[0].astype(f32)
    keep[1] = keep_high[0] + high[0].astype(f32)


def add_third(keep, low, high, own, one, two, three):
    own[...] = keep[0, 0] + low[0].astype(f32)
    one[...] = (keep[1, 0] + low[1].astype(f32)).astype(bf16)
    two[...] = (keep[0, 1] + high[0].astype(f32)).astype(bf16)
    three[...] = (keep[1, 1] + high[1].astype(f32)).astype(bf16)


def add_final(own, one, two, three, out):
    out[...] = own[...] + one[...].astype(f32) + two[...].astype(f32) + three[...].astype(f32)


def gather_custom(chunk_a, chunk_b, chunk_c, silu_send, head):
    block = chunk_a.shape[0]
    pair = shaped((2, block, D), bf16)

    def along(chunk):
        return [chunk] + [swap_tensor(chunk, j) for j in (1, 2, 3)]

    def pack(blocks):
        flat = pl.BlockSpec((block, D), lambda i: (0, 0))
        both = pl.BlockSpec((2, block, D), lambda i: (0, 0, 0))
        return run_blocks(pack_pairs, (1,), [(v, flat) for v in blocks], [(pair, both)] * 2)

    def first(packed):
        low, high = packed
        got = [swap_dp(low, 2), swap_dp(high, 4), swap_dp(low, 4), swap_dp(high, 2)]
        return [low, high, *got]

    def second(got):
        low, high, low_x, high_y, low_y, high_x = got
        low_xy, high_xy = swap_dp(low_x, 4), swap_dp(high_y, 2)
        return [low, low_x, low_y, low_xy, high, high_x, high_y, high_xy]

    def third(held):
        return [piece for part in held for piece in (part, swap_dp(part, 1))]

    z_a, z_b, z_c = along(chunk_a), along(chunk_b), along(chunk_c)
    pack_a, pack_b, pack_c = pack(z_a), pack(z_b), pack(z_c)
    _, silu_send = barrier(pack_b, silu_send)
    context = head(silu_send)
    three_a, three_b, three_c = [
        third(second(first(packed)))
        for packed in (pack_a, pack_b, pack_c)
    ]
    return three_a, three_b, three_c, context


def add_one(mine, got):
    block = got.shape[1] // 4
    wide = shaped((2, 2, block, D), bf16)
    keep = shaped(wide.shape, f32)
    out = pl.BlockSpec((None, 2, block, D), lambda j: (j, 0, 0, 0))

    def slot(value, first):
        return value, pl.BlockSpec((None,) + value.shape[1:], lambda j: (first + j, 0, 0))

    operands = []
    for turn, right in mine:
        operands.append((turn, pl.BlockSpec((HALF, SEQ), lambda j: (0, 0))))
        operands += [slot(right, 0), slot(right, 2)]
        if len(operands) == 3:
            operands += [slot(got, 0), slot(got, 2)]
    return run_blocks(
        add_first,
        (2,),
        operands,
        [(wide, out), (wide, out), (keep, out), (keep, out)],
        flops=2 * SEQ * HALF * D * 4,
    )


def send_one(state):
    return swap_dp(state[0], 2), swap_dp(state[1], 4)


def add_two(state, got):
    block = state[2].shape[2]
    pair = shaped((2, block, D), bf16)
    wide = pl.BlockSpec((None, 2, block, D), lambda j: (j, 0, 0, 0))
    one = pl.BlockSpec((None, block, D), lambda j: (j, 0, 0))
    return run_blocks(
        add_second,
        (2,),
        [(v, wide) for v in (state[2], state[3], *got)],
        [(pair, one), (pair, one), (shaped((2, 2, block, D), f32), wide)],
    )


def send_two(state):
    return swap_dp(state[0], 4), swap_dp(state[1], 2)


def add_three(state, got):
    block = state[2].shape[2]
    half = D // 2
    one = shaped((block, D), bf16)
    keep = pl.BlockSpec((2, 2, block, half), lambda i: (0, 0, 0, i))
    pair = pl.BlockSpec((2, block, half), lambda i: (0, 0, i))
    flat = pl.BlockSpec((block, half), lambda i: (0, i))
    return run_blocks(
        add_third,
        (2,),
        [(state[2], keep), (got[0], pair), (got[1], pair)],
        [(shaped((block, D), f32), flat), (one, flat), (one, flat), (one, flat)],
    )


def send_three(state):
    return [swap_tensor(state[j], j) for j in (1, 2, 3)]


def send_core(away):
    return swap_dp(away, 1)


def add_last(state, got):
    flat = pl.BlockSpec(state[0].shape, lambda i: (0, 0))
    return run_blocks(
        add_final,
        (1,),
        [(v, flat) for v in (state[0], *got)],
        [(shaped(state[0].shape, f32), flat)],
    )[0]


def gather_plain(*chunks):
    full = []
    for chunk in chunks:
        near = by_slot(lax.all_gather(chunk, "tensor", axis=0))
        full.append([lax.all_gather(near, "dp", axis=1, tiled=True)])
    return full


def scatter_plain(away, mine):
    parts = [
        jnp.einsum("fr,trc->tfc", turn[:HALF], right, preferred_element_type=f32)
        for turn, right in mine
    ]
    if len(parts) > 1:
        parts[0] = parts[0][:, :, : D - parts[1].shape[2]]
    grad = jnp.concatenate([jnp.concatenate(parts, axis=2), away.astype(f32)], axis=1)
    grad = by_slot(grad)
    near = lax.psum_scatter(grad, "tensor", scatter_dimension=0, tiled=True)[0]
    return lax.psum_scatter(near, "dp", scatter_dimension=0, tiled=True)


def body(
    tokens,
    conditioning,
    cotangent,
    w_ada,
    b_ada,
    w_qkv,
    b_qv,
    w_out,
    b_out,
    w_fc1,
    b_fc1,
    w_fc2,
    b_fc2,
):
    n_d = lax.axis_size("dp")
    n_t = lax.axis_size("tensor")
    devices = n_d * n_t
    dp_at = lax.axis_index("dp")
    t_at = lax.axis_index("tensor")
    custom = n_d == 8 and n_t == 4
    block = w_fc1.shape[0]
    width = w_qkv.shape[2]
    ada_cols = w_ada.shape[1]
    group = conditioning.shape[0]
    exact = lax.Precision.HIGHEST

    if custom:
        order = feature_order(block)
        shuffle = lambda v: jnp.dot(v, order, precision=exact)
        restore = lambda v: lax.dot_general(v, order, (((1,), (1,)), ((), ())), precision=exact)
    else:
        shuffle = restore = lambda v: v

    chunk_a = jnp.concatenate([w_qkv.reshape(block, 3 * width), w_out.T], axis=1)
    sig_cond = jax.nn.sigmoid(conditioning)
    silu_cond = (conditioning * sig_cond).astype(bf16)
    silu_send = silu_cond.reshape(group, n_d, block).transpose(1, 0, 2)

    def head(silu_send):
        silu_rows = lax.all_to_all(silu_send, "dp", split_axis=0, concat_axis=0, tiled=True)
        silu_rows = silu_rows.reshape(n_d * group, block)
        mod_part = jnp.dot(silu_rows, w_ada, preferred_element_type=f32)
        mod_part = mod_part + (dp_at == 0).astype(f32) * b_ada
        bias_own = jnp.concatenate([b_qv.reshape(-1), b_fc1])
        head_send = jnp.concatenate(
            [mod_part, jnp.broadcast_to(bias_own, (devices, bias_own.shape[0]))], axis=1
        )
        head_got = lax.all_to_all(head_send, BOTH, split_axis=0, concat_axis=0, tiled=True)
        head_got = head_got.reshape(n_d, n_t, head_send.shape[1])
        modulation = jnp.sum(head_got[:, :, :ada_cols], axis=0).reshape(6, D)
        mods = shuffle(jnp.concatenate([modulation, b_out[None], b_fc2[None]], axis=0))
        bias_all = by_slot(head_got[0, :, ada_cols:])
        none = jnp.zeros((n_t, width), f32)
        bias_a = jnp.concatenate(
            [bias_all[:, :width], none, bias_all[:, width : 2 * width], none], axis=1
        )[:, None]
        bias_b = bias_all[:, None, 2 * width :]
        return silu_rows, mods, bias_a, bias_b

    chunks = (chunk_a, w_fc1, w_fc2.T)
    if custom:
        full_a, full_b, full_c, context = gather_custom(*chunks, silu_send, head)
    else:
        full_a, full_b, full_c = gather_plain(*chunks)
        context = head(silu_send)
    silu_rows, mods, bias_a, bias_b = context
    tokens_s = shuffle(tokens)
    cot = shuffle(cotangent)
    rows_f = shaped((SEQ, D), f32)
    rows_b = shaped((SEQ, D), bf16)
    slots_b = shaped((n_t, SEQ, D), bf16)
    sums_f = shaped((n_t, 1, D), f32)
    away_b = shaped((n_t, HALF, D), bf16)
    turn_b = shaped((D, SEQ), bf16)
    vectors = shaped((8, D), f32)
    unit = 2 * SEQ * D * D * n_t

    def attend(full):
        return run(
            attention_forward,
            (tokens_s, mods, bias_a),
            (full,),
            (rows_b, slots_b, shaped((n_t, SEQ, width), bf16), rows_f, rows_f, rows_b),
            flops=2 * unit,
        )

    forward = attend(full_a)
    hidden_one, proj, attended, branch_one, middle, hidden_two = forward
    act, slope, grad_two, away_c, turn_two = run(
        hidden_units,
        (hidden_two, cot, mods, bias_b),
        (full_b,),
        (slots_b, shaped(slots_b.shape, f32), rows_b, away_b, turn_b),
        flops=2 * unit,
    )
    mine_c = ((turn_two, act),)
    if custom:
        got_c = send_core(away_c)
        state_c = add_one(mine_c, got_c)
        _, hidden_two = barrier(state_c, hidden_two)
        got_c = send_one(state_c)
    grad_pre, sums_b, away_b1, turn_hidden = run(
        hidden_back,
        (hidden_two, grad_two, slope),
        (full_c,),
        (slots_b, sums_f, away_b, turn_b),
        flops=2 * unit,
    )
    mine_b = ((turn_hidden, grad_pre),)
    if custom:
        got_b = send_core(away_b1)
        got_c, grad_pre = barrier(got_c, grad_pre)
        state_c = add_two(state_c, got_c)
        _, act = barrier(state_c, act)
        got_c = send_two(state_c)
    output, grad_middle, grad_one, rows_mid = run(
        middle_back,
        (act, grad_pre, cot, middle, branch_one, grad_two, mods),
        (full_c, full_b),
        (rows_f, rows_f, rows_b, vectors),
        scratch=[pltpu.VMEM((SEQ, D), f32)] * 2,
        flops=2 * unit,
    )
    if custom:
        got_b, got_c, grad_one = barrier(got_b, got_c, grad_one)
        state_b = add_one(mine_b, got_b)
        state_c = add_three(state_c, got_c)
        _, _, grad_one, output = barrier(state_c, state_b, grad_one, output)
        got_b, got_c = send_one(state_b), send_three(state_c)
    output = restore(output)
    away_a, grads_a, sums_a, back, turn_one, turn_grad = run(
        attention_back,
        (grad_one, proj, attended, hidden_one),
        (full_a,),
        (away_b, slots_b, sums_f, rows_f, turn_b, turn_b),
        scratch=[pltpu.VMEM((SEQ, D), f32)],
        flops=3 * unit,
    )
    mine_a = ((turn_one, grads_a), (turn_grad, attended))
    if custom:
        got_a = send_core(away_a)
        got_b, grads_a = barrier(got_b, grads_a)
        mine_a = ((turn_one, grads_a), (turn_grad, attended))
        state_b = add_two(state_b, got_b)
        got_b = send_two(state_b)
        state_a = add_one(mine_a, got_a)
        got_a = send_one(state_a)
        _, got_c, got_b, back = barrier(state_a, got_c, got_b, back)
        state_b = add_three(state_b, got_b)
        _, back = barrier(state_b, back)
        got_b = send_three(state_b)
    grad_tokens, rows_top = run(
        token_back, (tokens_s, grad_middle, back, mods), (), (rows_f, vectors)
    )
    if custom:
        grad_tokens, rows_top, got_a = barrier(grad_tokens, rows_top, got_a)
        state_a = add_two(state_a, got_a)
        _, got_b, got_c, grad_tokens, rows_top = barrier(
            state_a, got_b, got_c, grad_tokens, rows_top
        )
        got_a = send_two(state_a)
        g_fc2 = add_last(state_c, got_c).T
        g_fc1 = add_last(state_b, got_b)
        state_a = add_three(state_a, got_a)
        got_a = send_three(state_a)
        g_chunk_a = add_last(state_a, got_a)
    else:
        g_fc2 = scatter_plain(away_c, mine_c).T
        g_fc1 = scatter_plain(away_b1, mine_b)
        g_chunk_a = scatter_plain(away_a, mine_a)
    g_qkv = g_chunk_a[:, : 3 * width].reshape(block, 3, width)
    g_out = g_chunk_a[:, 3 * width :].T
    grad_tokens = restore(grad_tokens)

    small = restore(rows_mid + rows_top)
    sums_a = by_slot(sums_a[:, 0])
    biases = jnp.concatenate(
        [
            sums_a[:, :width].reshape(-1),
            sums_a[:, 2 * width : 3 * width].reshape(-1),
            by_slot(sums_b[:, 0]).reshape(-1),
            small[6],
            small[7],
        ]
    )
    piece = biases.shape[0] // devices
    mod_send = jnp.broadcast_to(small[:6].reshape(1, n_t, ada_cols), (n_d, n_t, ada_cols))
    first_send = jnp.concatenate(
        [mod_send, biases.reshape(n_d, n_t, piece)], axis=2
    ).reshape(devices, ada_cols + piece)
    first_got = lax.all_to_all(first_send, BOTH, split_axis=0, concat_axis=0, tiled=True)
    grad_mod = first_got[:, :ada_cols]
    bias_piece = jnp.sum(first_got[:, ada_cols:], axis=0)
    gb_ada = jnp.sum(grad_mod, axis=0)
    g_ada = jnp.dot(silu_rows.astype(f32).T, grad_mod, precision=exact)
    silu_part = lax.dot_general(
        grad_mod, w_ada.astype(f32), (((1,), (1,)), ((), ())), precision=exact
    )
    second_send = jnp.concatenate(
        [
            jnp.broadcast_to(silu_part.reshape(n_d, 1, group * block), (n_d, n_t, group * block)),
            jnp.broadcast_to(bias_piece, (n_d, n_t, piece)),
        ],
        axis=2,
    ).reshape(devices, group * block + piece)
    second_got = lax.all_to_all(second_send, BOTH, split_axis=0, concat_axis=0, tiled=True)
    grad_silu = jnp.sum(
        second_got[:, : group * block].reshape(n_d, n_t, group, block), axis=1
    )
    grad_silu = grad_silu.transpose(1, 0, 2).reshape(group, D)
    grad_cond = grad_silu * sig_cond * (1.0 + conditioning * (1.0 - sig_cond))
    summed = second_got[:, group * block :].reshape(-1)
    qv_size = n_t * width
    fc1_own = w_fc1.shape[1]
    fc1_size = n_t * fc1_own
    gb_qv = lax.dynamic_index_in_dim(
        summed[: 2 * qv_size].reshape(2, n_t, width), t_at, 1, keepdims=False
    )
    gb_fc1 = lax.dynamic_index_in_dim(
        summed[2 * qv_size : 2 * qv_size + fc1_size].reshape(n_t, fc1_own), t_at, 0, keepdims=False
    )
    gb_out = summed[2 * qv_size + fc1_size : 2 * qv_size + fc1_size + D]
    gb_fc2 = summed[2 * qv_size + fc1_size + D :]
    return (
        output,
        grad_tokens,
        grad_cond,
        g_ada,
        gb_ada,
        g_qkv,
        gb_qv,
        g_out,
        gb_out,
        g_fc1,
        gb_fc1,
        g_fc2,
        gb_fc2,
    )


def solution(mesh):
    specs = (
        P(("dp", "tensor"), None),
        P("dp", None),
        P(("dp", "tensor"), None),
        P("dp", "tensor"),
        P("tensor"),
        P("dp", None, "tensor"),
        P(None, "tensor"),
        P("tensor", "dp"),
        P(),
        P("dp", "tensor"),
        P("tensor"),
        P("tensor", "dp"),
        P(),
    )
    out_specs = (specs[0], specs[0], specs[1]) + specs[3:]
    return jax.shard_map(body, mesh=mesh, in_specs=specs, out_specs=out_specs, check_vma=False)
```

```python
import jax
import jax.numpy as jnp
from jax import lax
from jax.experimental import pallas as pl
from jax.experimental.pallas import tpu as pltpu
from jax.sharding import PartitionSpec as P


D = 768
HD = 64
SEQ = 256


epsilon = 1e-06
gelu_coef = 0.7978845608028654
cube_coef = 0.044715
f32 = jnp.float32
bf16 = jnp.bfloat16
BOTH = ("dp", "tensor")


def gelu_parts(pre_act):
    inner_arg = gelu_coef * (pre_act + cube_coef * pre_act * pre_act * pre_act)
    tangent = jnp.tanh(inner_arg)
    result = 0.5 * pre_act * (1.0 + tangent)
    gelu_slope = 0.5 * (1.0 + tangent) + 0.5 * pre_act * (1.0 - tangent * tangent) * gelu_coef * (
        1.0 + 3.0 * cube_coef * pre_act * pre_act
    )
    return (result, gelu_slope)


def normalize(rows_in):
    center = rows_in - jnp.mean(rows_in, axis=-1, keepdims=True)
    inv_std = lax.rsqrt(jnp.mean(center * center, axis=-1, keepdims=True) + epsilon)
    return (center * inv_std, inv_std)


def norm_back(grad_normed, normed, inv_std):
    return inv_std * (
        grad_normed
        - jnp.mean(grad_normed, axis=-1, keepdims=True)
        - normed * jnp.mean(grad_normed * normed, axis=-1, keepdims=True)
    )


def barrier(*values):
    return lax.optimization_barrier(values)


def swap_dp(value, bit):
    size = lax.axis_size("dp")
    return lax.ppermute(value, "dp", [(i, i ^ bit) for i in range(size)])


def swap_tensor(value, bit):
    size = lax.axis_size("tensor")
    return lax.ppermute(value, "tensor", [(i, i ^ bit) for i in range(size)])


HALF = D // 2


def feature_order(block):
    me = lax.axis_index("dp")
    place = lax.broadcasted_iota(jnp.int32, (D, D), 1)
    source = lax.broadcasted_iota(jnp.int32, (D, D), 0)
    slot = place // block
    flip = ((slot // 2) % 2) * 4 + (slot % 2) * 2 + slot // 4
    return ((me ^ flip) * block + place % block == source).astype(f32)


def by_slot(value):
    me = lax.axis_index("tensor")
    return jnp.stack(
        [lax.dynamic_index_in_dim(value, me ^ j, 0, keepdims=False) for j in range(4)]
    )


VM = pl.BlockSpec(memory_space=pltpu.VMEM)
ANY = pl.BlockSpec(memory_space=pl.ANY)


def shaped(shape, kind):
    return jax.ShapeDtypeStruct(shape, kind)


FULL_GRANT = ("attention_back", "token_back", "add_second_b", "add_third_b", "add_first_a", "add_second_a", "add_third_a")


def granted(name):
    if name in FULL_GRANT:
        return pltpu.CompilerParams()
    small = name.startswith(("add_", "pack_"))
    return pltpu.CompilerParams(vmem_limit_bytes=(12 if small else 24) << 20)


def spec_of(shape):
    if len(shape) == 3 and shape[0] == 4:
        return pl.BlockSpec((None,) + tuple(shape[1:]), lambda j: (j, 0, 0))
    return pl.BlockSpec(tuple(shape), lambda j: (0,) * len(shape))


def run(kernel, name, operands, pieces, outs, scratch=(), flops=0):
    flat = [ref for group in pieces for ref in group]
    loads = [pltpu.VMEM((4, D, D), bf16) for _ in pieces]
    sems = [pltpu.SemaphoreType.DMA((4 * max(len(group) // 2, 1),)) for group in pieces]
    moved = sum(v.size * v.dtype.itemsize for v in list(operands) + flat)
    moved += sum(int(o.size) * o.dtype.itemsize for o in outs)

    def wrapped(*refs):
        n_in, n_flat, n_out = len(operands), len(flat), len(outs)
        ins = refs[:n_in]
        raw = refs[n_in : n_in + n_flat]
        out_refs = refs[n_in + n_flat : n_in + n_flat + n_out]
        rest = refs[n_in + n_flat + n_out :]
        chunks, at = [], 0
        for which, group in enumerate(pieces):
            chunks.append(
                start_load(raw[at : at + len(group)], rest[which], rest[len(pieces) + which])
            )
            at += len(group)
        kernel(*ins, *chunks, *out_refs, *rest[2 * len(pieces) :])

    return pl.pallas_call(
        wrapped,
        grid=(4,),
        out_shape=tuple(outs),
        in_specs=[spec_of(v.shape) for v in operands] + [ANY] * len(flat),
        out_specs=tuple(spec_of(o.shape) for o in outs),
        scratch_shapes=loads + sems + list(scratch),
        compiler_params=granted(name),
        cost_estimate=pl.CostEstimate(flops=flops, bytes_accessed=moved, transcendentals=0),
    )(*operands, *flat)


def run_blocks(kernel, name, grid, operands, outs, flops=0):
    moved = sum(v.size * v.dtype.itemsize for v, _ in operands)
    moved += sum(int(o.size) * o.dtype.itemsize for o, _ in outs)
    return pl.pallas_call(
        kernel,
        grid=grid,
        out_shape=tuple(o for o, _ in outs),
        in_specs=[spec for _, spec in operands],
        out_specs=tuple(spec for _, spec in outs),
        compiler_params=granted(name),
        cost_estimate=pl.CostEstimate(flops=flops, bytes_accessed=moved, transcendentals=0),
    )(*[v for v, _ in operands])


def start_load(refs, full, sems):
    step = pl.program_id(0)
    count = 1 if len(refs) == 1 else 8
    size = D // count

    @pl.when(step == 0)
    def _():
        for j in range(4):
            if count == 1:
                pltpu.make_async_copy(refs[0].at[j], full.at[j], sems.at[j]).start()
                continue
            for p in range(8):
                source = refs[((j // 2) * 4 + p % 4) * 2 + p // 4]
                pltpu.make_async_copy(
                    source.at[j % 2], full.at[j, pl.ds(p * size, size)], sems.at[j * 8 + p]
                ).start()

    def get():
        for p in range(count):
            pltpu.make_async_copy(
                refs[0].at[0], full.at[step, pl.ds(p * size, size)], sems.at[step * count + p]
            ).wait()
        return full[step]

    return get


def opening(act):
    pl.when(pl.program_id(0) == 0)(act)


def closing(act):
    pl.when(pl.program_id(0) == 3)(act)


def dot(a, b):
    return jnp.dot(a, b, preferred_element_type=f32)


def dot_nt(a, b):
    return lax.dot_general(a, b, (((1,), (1,)), ((), ())), preferred_element_type=f32)


def turned(value):
    return value.astype(f32).T.astype(bf16)


def total(value):
    return jnp.sum(value, axis=0, keepdims=True)


def soft(q, k):
    scores = dot_nt(k, q) * (HD ** (-0.5))
    top = jnp.max(scores, axis=0, keepdims=True)
    log_total = top + jnp.log(jnp.sum(jnp.exp(scores - top), axis=0, keepdims=True))
    return jnp.exp(scores - log_total)


def attention_forward(tokens, mods, bias, chunk, hidden, proj, att, branch, middle, hidden_two):
    @opening
    def _():
        normed, _ = normalize(tokens[...])
        hidden[...] = (normed * (1.0 + mods[1:2]) + mods[0:1]).astype(bf16)
        branch[...] = jnp.broadcast_to(mods[6:7], branch.shape)

    width = att.shape[1]
    weight = chunk()
    now = (dot(hidden[...], weight) + bias[...]).astype(bf16)
    proj[...] = now
    values = turned(now[:, 2 * width : 3 * width])
    heads = []
    for lo in range(0, width, HD):
        probs = soft(now[:, lo : lo + HD], now[:, width + lo : width + lo + HD])
        heads.append(dot(values[lo : lo + HD], probs.astype(bf16)))
    att[...] = jnp.concatenate(heads, axis=0).T.astype(bf16)
    branch[...] += dot_nt(att[...], weight[:, 3 * width :])

    @closing
    def _():
        middle_now = tokens[...] + mods[2:3] * branch[...]
        middle[...] = middle_now
        normed_two, _ = normalize(middle_now)
        hidden_two[...] = (normed_two * (1.0 + mods[4:5]) + mods[3:4]).astype(bf16)


def hidden_units(
    hidden_two, cot, mods, bias, chunk, act, slope, grad_two, away, grad_turned
):
    @opening
    def _():
        grad_two[...] = (cot[...] * mods[5:6]).astype(bf16)
        grad_turned[...] = turned(grad_two[...])

    value, slope_now = gelu_parts(dot(hidden_two[...], chunk()) + bias[...])
    low = value.astype(bf16)
    act[...] = low
    slope[...] = slope_now
    away[...] = dot(grad_turned[HALF:], low).astype(bf16)


def hidden_back(hidden_two, grad_two, slope, chunk, grad_pre, sums, away, hidden_turned):
    @opening
    def _():
        hidden_turned[...] = turned(hidden_two[...])

    grad = dot(grad_two[...], chunk()) * slope[...]
    sums[...] = total(grad)
    low = grad.astype(bf16)
    grad_pre[...] = low
    away[...] = dot(hidden_turned[HALF:], low).astype(bf16)


def restored(value, order):
    high = value.astype(bf16)
    rest = value - high.astype(f32)
    middle = rest.astype(bf16)
    low = (rest - middle.astype(f32)).astype(bf16)
    return dot_nt(high, order) + dot_nt(middle, order) + dot_nt(low, order)


def block_output(act, cot, middle, mods, order, chunk, out, gate, two):
    @opening
    def _():
        two[...] = jnp.broadcast_to(mods[7:8], two.shape)

    two[...] += dot_nt(act[...], chunk())

    @closing
    def _():
        out[...] = restored(middle[...] + mods[5:6] * two[...], order[...])
        gate[...] = jnp.zeros_like(gate)
        gate[5:6] = total(cot[...] * two[...])


def middle_back(
    grad_pre, cot, middle, branch_one, grad_two, mods, chunk,
    grad_middle, grad_one, rows, back,
):
    @opening
    def _():
        back[...] = jnp.zeros_like(back)

    back[...] += dot_nt(grad_pre[...], chunk())

    @closing
    def _():
        grad_hidden = back[...]
        normed, inv = normalize(middle[...])
        grad = cot[...] + norm_back(grad_hidden * (1.0 + mods[4:5]), normed, inv)
        grad_middle[...] = grad
        grad_one[...] = (grad * mods[2:3]).astype(bf16)
        rows[...] = jnp.zeros_like(rows)
        rows[2:3] = total(grad * branch_one[...])
        rows[3:4] = total(grad_hidden)
        rows[4:5] = total(grad_hidden * normed)
        rows[6:7] = total(grad_one[...].astype(f32))
        rows[7:8] = total(grad_two[...].astype(f32))


def attention_back(
    grad_one, proj, att, hidden, chunk, away, grads, sums, back, hidden_turned, grad_turned, wide
):
    @opening
    def _():
        wide[...] = jnp.zeros_like(wide)
        back[...] = jnp.zeros_like(back)
        hidden_turned[...] = turned(hidden[...])
        grad_turned[...] = turned(grad_one[...])

    width = att.shape[1]
    weight = chunk()
    now = proj[...]
    grad_att = dot(grad_one[...], weight[:, 3 * width :]).astype(bf16)
    keys = turned(now[:, width : 2 * width])
    query_grads = []
    for lo in range(0, width, HD):
        hi = lo + HD
        q = now[:, lo:hi]
        g = grad_att[:, lo:hi]
        probs = soft(q, now[:, width + lo : width + hi])
        wide[:, 2 * width + lo : 2 * width + hi] = dot(probs.astype(bf16), g)
        grad_probs = dot_nt(now[:, 2 * width + lo : 2 * width + hi], g)
        inner = jnp.sum(probs * grad_probs, axis=0, keepdims=True)
        scores = (probs * (grad_probs - inner) * (HD ** (-0.5))).astype(bf16)
        query_grads.append(dot(keys[lo:hi], scores))
        wide[:, width + lo : width + hi] = dot(scores, q)
    wide[:, :width] = jnp.concatenate(query_grads, axis=0).T
    sums[...] = total(wide[...])
    grad_proj = wide[...].astype(bf16)
    grads[...] = grad_proj
    away[...] = dot(hidden_turned[HALF:], grad_proj).astype(bf16)
    away[:, 3 * width :] = dot(grad_turned[HALF:], att[...]).astype(bf16)
    back[...] += dot_nt(grad_proj, weight)


def token_back(tokens, grad_middle, back, mods, order, grad_tokens, rows):
    @opening
    def _():
        normed, inv = normalize(tokens[...])
        rows[...] = jnp.zeros_like(rows)
        rows[0:1] = total(back[...])
        rows[1:2] = total(back[...] * normed)
        grad = grad_middle[...] + norm_back(back[...] * (1.0 + mods[1:2]), normed, inv)
        grad_tokens[...] = restored(grad, order[...])


def pack_pairs(first, second, third, fourth, low, high):
    low[0] = first[...]
    low[1] = second[...]
    high[0] = third[...]
    high[1] = fourth[...]


def add_first(*refs):
    *ins, send_low, send_high, keep_low, keep_high = refs
    turn, low, high, low_got, high_got = ins[:5]
    low_now = dot(turn[...], low[...])
    high_now = dot(turn[...], high[...])
    if len(ins) > 5:
        turn_two, low_two, high_two = ins[5:]
        cut = D - low_two.shape[1]
        low_now = jnp.concatenate([low_now[:, :cut], dot(turn_two[...], low_two[...])], axis=1)
        high_now = jnp.concatenate([high_now[:, :cut], dot(turn_two[...], high_two[...])], axis=1)
    low_now = low_now + low_got[...].astype(f32)
    high_now = high_now + high_got[...].astype(f32)
    block = keep_low.shape[1]
    for k in range(2):
        at = 2 * k * block
        keep_low[k] = low_now[at : at + block]
        send_low[k] = low_now[at + block : at + 2 * block].astype(bf16)
        at = k * block
        keep_high[k] = high_now[at : at + block]
        send_high[k] = high_now[at + 2 * block : at + 3 * block].astype(bf16)


def add_second(keep_low, keep_high, low, high, send_low, send_high, keep):
    send_low[...] = (keep_low[1] + low[1].astype(f32)).astype(bf16)
    send_high[...] = (keep_high[1] + high[1].astype(f32)).astype(bf16)
    keep[0] = keep_low[0] + low[0].astype(f32)
    keep[1] = keep_high[0] + high[0].astype(f32)


def add_third(keep, low, high, own, one, two, three):
    own[...] = keep[0, 0] + low[0].astype(f32)
    one[...] = (keep[1, 0] + low[1].astype(f32)).astype(bf16)
    two[...] = (keep[0, 1] + high[0].astype(f32)).astype(bf16)
    three[...] = (keep[1, 1] + high[1].astype(f32)).astype(bf16)


def add_final(own, one, two, three, out):
    out[...] = own[...] + one[...].astype(f32) + two[...].astype(f32) + three[...].astype(f32)


def gather_custom(chunk_a, chunk_b, chunk_c, head_send, finish, shuffled):
    block = chunk_a.shape[0]
    pair = shaped((2, block, D), bf16)

    def along(chunk):
        return [chunk] + [swap_tensor(chunk, j) for j in (1, 2, 3)]

    def pack(blocks, tag):
        flat = pl.BlockSpec((block, D), lambda i: (0, 0))
        both = pl.BlockSpec((2, block, D), lambda i: (0, 0, 0))
        return run_blocks(
            pack_pairs, "pack_" + tag, (1,), [(v, flat) for v in blocks], [(pair, both)] * 2
        )

    def first(packed):
        low, high = packed
        got = [swap_dp(low, 2), swap_dp(high, 4), swap_dp(low, 4), swap_dp(high, 2)]
        return [low, high, *got]

    def second(got):
        low, high, low_x, high_y, low_y, high_x = got
        low_xy, high_xy = swap_dp(low_x, 4), swap_dp(high_y, 2)
        return [low, low_x, low_y, low_xy, high, high_x, high_y, high_xy]

    def third(held):
        return [piece for part in held for piece in (part, swap_dp(part, 1))]

    context = finish(head_send)
    z_a, z_b, z_c = along(chunk_a), along(chunk_b), along(chunk_c)
    pack_a, pack_b = pack(z_a, "a"), pack(z_b, "b")
    z_c, _ = barrier(z_c, shuffled)
    pack_c = pack(z_c, "c")
    three_a, three_b, three_c = [
        third(second(first(packed)))
        for packed in (pack_a, pack_b, pack_c)
    ]
    return three_a, three_b, three_c, context


def add_one(mine, got, tag):
    block = got.shape[1] // 4
    wide = shaped((2, 2, block, D), bf16)
    keep = shaped(wide.shape, f32)
    out = pl.BlockSpec((None, 2, block, D), lambda j: (j, 0, 0, 0))

    def slot(value, first):
        return value, pl.BlockSpec((None,) + value.shape[1:], lambda j: (first + j, 0, 0))

    operands = []
    for turn, right in mine:
        operands.append((turn, pl.BlockSpec((HALF, SEQ), lambda j: (0, 0))))
        operands += [slot(right, 0), slot(right, 2)]
        if len(operands) == 3:
            operands += [slot(got, 0), slot(got, 2)]
    return run_blocks(
        add_first,
        "add_first_" + tag,
        (2,),
        operands,
        [(wide, out), (wide, out), (keep, out), (keep, out)],
        flops=2 * SEQ * HALF * D * 4,
    )


def send_one(state):
    return swap_dp(state[0], 2), swap_dp(state[1], 4)


def add_two(state, got, tag):
    block = state[2].shape[2]
    pair = shaped((2, block, D), bf16)
    wide = pl.BlockSpec((None, 2, block, D), lambda j: (j, 0, 0, 0))
    one = pl.BlockSpec((None, block, D), lambda j: (j, 0, 0))
    return run_blocks(
        add_second,
        "add_second_" + tag,
        (2,),
        [(v, wide) for v in (state[2], state[3], *got)],
        [(pair, one), (pair, one), (shaped((2, 2, block, D), f32), wide)],
    )


def send_two(state):
    return swap_dp(state[0], 4), swap_dp(state[1], 2)


def add_three(state, got, tag):
    block = state[2].shape[2]
    half = D // 2
    one = shaped((block, D), bf16)
    keep = pl.BlockSpec((2, 2, block, half), lambda i: (0, 0, 0, i))
    pair = pl.BlockSpec((2, block, half), lambda i: (0, 0, i))
    flat = pl.BlockSpec((block, half), lambda i: (0, i))
    return run_blocks(
        add_third,
        "add_third_" + tag,
        (2,),
        [(state[2], keep), (got[0], pair), (got[1], pair)],
        [(shaped((block, D), f32), flat), (one, flat), (one, flat), (one, flat)],
    )


def send_three(state):
    return [swap_tensor(state[j], j) for j in (1, 2, 3)]


def send_core(away):
    return swap_dp(away, 1)


def add_last(state, got, tag):
    flat = pl.BlockSpec(state[0].shape, lambda i: (0, 0))
    return run_blocks(
        add_final,
        "add_final_" + tag,
        (1,),
        [(v, flat) for v in (state[0], *got)],
        [(shaped(state[0].shape, f32), flat)],
    )[0]


def gather_plain(*chunks):
    full = []
    for chunk in chunks:
        near = by_slot(lax.all_gather(chunk, "tensor", axis=0))
        full.append([lax.all_gather(near, "dp", axis=1, tiled=True)])
    return full


def scatter_plain(away, mine):
    parts = [
        jnp.einsum("fr,trc->tfc", turn[:HALF], right, preferred_element_type=f32)
        for turn, right in mine
    ]
    if len(parts) > 1:
        parts[0] = parts[0][:, :, : D - parts[1].shape[2]]
    grad = jnp.concatenate([jnp.concatenate(parts, axis=2), away.astype(f32)], axis=1)
    grad = by_slot(grad)
    near = lax.psum_scatter(grad, "tensor", scatter_dimension=0, tiled=True)[0]
    return lax.psum_scatter(near, "dp", scatter_dimension=0, tiled=True)


def body(
    tokens,
    conditioning,
    cotangent,
    w_ada,
    b_ada,
    w_qkv,
    b_qv,
    w_out,
    b_out,
    w_fc1,
    b_fc1,
    w_fc2,
    b_fc2,
):
    n_d = lax.axis_size("dp")
    n_t = lax.axis_size("tensor")
    devices = n_d * n_t
    dp_at = lax.axis_index("dp")
    t_at = lax.axis_index("tensor")
    custom = n_d == 8 and n_t == 4
    block = w_fc1.shape[0]
    width = w_qkv.shape[2]
    ada_cols = w_ada.shape[1]
    group = conditioning.shape[0]
    exact = lax.Precision.HIGHEST

    if custom:
        order = feature_order(block)
        order_low = order.astype(bf16)
        shuffle = lambda v: jnp.dot(v, order, precision=exact)
        restore = lambda v: lax.dot_general(v, order, (((1,), (1,)), ((), ())), precision=exact)
    else:
        shuffle = restore = lambda v: v
        order_low = jnp.eye(D, dtype=bf16)

    chunk_a = jnp.concatenate([w_qkv.reshape(block, 3 * width), w_out.T], axis=1)
    sig_cond = jax.nn.sigmoid(conditioning)
    silu_cond = (conditioning * sig_cond).astype(bf16)
    silu_send = silu_cond.reshape(group, n_d, block).transpose(1, 0, 2)
    silu_rows = lax.all_to_all(silu_send, "dp", split_axis=0, concat_axis=0, tiled=True)
    silu_rows = silu_rows.reshape(n_d * group, block)
    mod_part = jnp.dot(silu_rows, w_ada, preferred_element_type=f32)
    mod_part = mod_part + (dp_at == 0).astype(f32) * b_ada
    bias_own = jnp.concatenate([b_qv.reshape(-1), b_fc1])
    head_send = jnp.concatenate(
        [mod_part, jnp.broadcast_to(bias_own, (devices, bias_own.shape[0]))], axis=1
    )

    def finish(head_send):
        head_got = lax.all_to_all(head_send, BOTH, split_axis=0, concat_axis=0, tiled=True)
        head_got = head_got.reshape(n_d, n_t, head_send.shape[1])
        modulation = jnp.sum(head_got[:, :, :ada_cols], axis=0).reshape(6, D)
        mods = shuffle(jnp.concatenate([modulation, b_out[None], b_fc2[None]], axis=0))
        bias_all = by_slot(head_got[0, :, ada_cols:])
        none = jnp.zeros((n_t, width), f32)
        bias_a = jnp.concatenate(
            [bias_all[:, :width], none, bias_all[:, width : 2 * width], none], axis=1
        )[:, None]
        bias_b = bias_all[:, None, 2 * width :]
        return mods, bias_a, bias_b

    chunks = (chunk_a, w_fc1, w_fc2.T)
    shuffled = (shuffle(tokens), shuffle(cotangent))
    if custom:
        full_a, full_b, full_c, context = gather_custom(
            *chunks, head_send, finish, shuffled
        )
    else:
        full_a, full_b, full_c = gather_plain(*chunks)
        context = finish(head_send)
    mods, bias_a, bias_b = context
    tokens_s, cot = shuffled
    rows_f = shaped((SEQ, D), f32)
    rows_b = shaped((SEQ, D), bf16)
    slots_b = shaped((n_t, SEQ, D), bf16)
    sums_f = shaped((n_t, 1, D), f32)
    away_b = shaped((n_t, HALF, D), bf16)
    turn_b = shaped((D, SEQ), bf16)
    vectors = shaped((8, D), f32)
    unit = 2 * SEQ * D * D * n_t

    def attend(full):
        return run(
            attention_forward,
            "attention_forward",
            (tokens_s, mods, bias_a),
            (full,),
            (rows_b, slots_b, shaped((n_t, SEQ, width), bf16), rows_f, rows_f, rows_b),
            flops=2 * unit,
        )

    forward = attend(full_a)
    hidden_one, proj, attended, branch_one, middle, hidden_two = forward
    act, slope, grad_two, away_c, turn_two = run(
        hidden_units,
        "hidden_units",
        (hidden_two, cot, mods, bias_b),
        (full_b,),
        (slots_b, shaped(slots_b.shape, f32), rows_b, away_b, turn_b),
        flops=2 * unit,
    )
    mine_c = ((turn_two, act),)
    if custom:
        got_c = send_core(away_c)
        state_c = add_one(mine_c, got_c, "c")
        _, hidden_two = barrier(state_c, hidden_two)
        got_c = send_one(state_c)
    grad_pre, sums_b, away_b1, turn_hidden = run(
        hidden_back,
        "hidden_back",
        (hidden_two, grad_two, slope),
        (full_c,),
        (slots_b, sums_f, away_b, turn_b),
        flops=2 * unit,
    )
    mine_b = ((turn_hidden, grad_pre),)
    if custom:
        got_b = send_core(away_b1)
        _, act = barrier(away_b1, act)
    output, row_gate = run(
        block_output,
        "block_output",
        (act, cot, middle, mods, order_low),
        (full_c,),
        (rows_f, vectors),
        scratch=[pltpu.VMEM((SEQ, D), f32)],
        flops=unit,
    )
    if custom:
        got_c, _ = barrier(got_c, row_gate)
        state_c = add_two(state_c, got_c, "c")
        _, grad_pre = barrier(state_c, grad_pre)
        got_c = send_two(state_c)
    grad_middle, grad_one, rows_mid = run(
        middle_back,
        "middle_back",
        (grad_pre, cot, middle, branch_one, grad_two, mods),
        (full_b,),
        (rows_f, rows_b, vectors),
        scratch=[pltpu.VMEM((SEQ, D), f32)],
        flops=unit,
    )
    if custom:
        got_b, got_c, grad_one = barrier(got_b, got_c, grad_one)
        state_b = add_one(mine_b, got_b, "b")
        state_c = add_three(state_c, got_c, "c")
        _, _, grad_one = barrier(state_c, state_b, grad_one)
        got_b, got_c = send_one(state_b), send_three(state_c)
    away_a, grads_a, sums_a, back, turn_one, turn_grad = run(
        attention_back,
        "attention_back",
        (grad_one, proj, attended, hidden_one),
        (full_a,),
        (away_b, slots_b, sums_f, rows_f, turn_b, turn_b),
        scratch=[pltpu.VMEM((SEQ, D), f32)],
        flops=3 * unit,
    )
    mine_a = ((turn_one, grads_a), (turn_grad, attended))
    if custom:
        got_a = send_core(away_a)
        got_b, grads_a = barrier(got_b, grads_a)
        mine_a = ((turn_one, grads_a), (turn_grad, attended))
        state_b = add_two(state_b, got_b, "b")
        got_b = send_two(state_b)
        state_a = add_one(mine_a, got_a, "a")
        got_a = send_one(state_a)
        _, got_c, got_b, back, sums_a, sums_b = barrier(
            state_a, got_c, got_b, back, sums_a, sums_b
        )
        state_b = add_three(state_b, got_b, "b")
        got_b = send_three(state_b)
    grad_tokens, rows_top = run(
        token_back,
        "token_back",
        (tokens_s, grad_middle, back, mods, order_low),
        (),
        (rows_f, vectors),
    )

    small = restore(rows_mid + rows_top + row_gate)
    sums_a = by_slot(sums_a[:, 0])
    biases = jnp.concatenate(
        [
            sums_a[:, :width].reshape(-1),
            sums_a[:, 2 * width : 3 * width].reshape(-1),
            by_slot(sums_b[:, 0]).reshape(-1),
            small[6],
            small[7],
        ]
    )
    piece = biases.shape[0] // devices
    mod_send = jnp.broadcast_to(small[:6].reshape(1, n_t, ada_cols), (n_d, n_t, ada_cols))
    first_send = jnp.concatenate(
        [mod_send, biases.reshape(n_d, n_t, piece)], axis=2
    ).reshape(devices, ada_cols + piece)
    if custom:
        got_a, _, _ = barrier(got_a, first_send, grad_tokens)
    first_got = lax.all_to_all(first_send, BOTH, split_axis=0, concat_axis=0, tiled=True)
    if custom:
        state_a = add_two(state_a, got_a, "a")
        got_a = send_two(state_a)
        state_a = add_three(state_a, got_a, "a")
        got_a = send_three(state_a)
        _, got_b, got_c, first_got = barrier(state_a, got_b, got_c, first_got)
        g_fc2 = add_last(state_c, got_c, "c").T
        g_fc1 = add_last(state_b, got_b, "b")
        g_chunk_a = add_last(state_a, got_a, "a")
    else:
        g_fc2 = scatter_plain(away_c, mine_c).T
        g_fc1 = scatter_plain(away_b1, mine_b)
        g_chunk_a = scatter_plain(away_a, mine_a)
    g_qkv = g_chunk_a[:, : 3 * width].reshape(block, 3, width)
    g_out = g_chunk_a[:, 3 * width :].T
    grad_mod = first_got[:, :ada_cols]
    bias_piece = jnp.sum(first_got[:, ada_cols:], axis=0)
    gb_ada = jnp.sum(grad_mod, axis=0)
    g_ada = jnp.dot(silu_rows.astype(f32).T, grad_mod, precision=exact)
    silu_part = lax.dot_general(
        grad_mod, w_ada.astype(f32), (((1,), (1,)), ((), ())), precision=exact
    )
    second_send = jnp.concatenate(
        [
            jnp.broadcast_to(silu_part.reshape(n_d, 1, group * block), (n_d, n_t, group * block)),
            jnp.broadcast_to(bias_piece, (n_d, n_t, piece)),
        ],
        axis=2,
    ).reshape(devices, group * block + piece)
    second_got = lax.all_to_all(second_send, BOTH, split_axis=0, concat_axis=0, tiled=True)
    grad_silu = jnp.sum(
        second_got[:, : group * block].reshape(n_d, n_t, group, block), axis=1
    )
    grad_silu = grad_silu.transpose(1, 0, 2).reshape(group, D)
    grad_cond = grad_silu * sig_cond * (1.0 + conditioning * (1.0 - sig_cond))
    summed = second_got[:, group * block :].reshape(-1)
    qv_size = n_t * width
    fc1_own = w_fc1.shape[1]
    fc1_size = n_t * fc1_own
    gb_qv = lax.dynamic_index_in_dim(
        summed[: 2 * qv_size].reshape(2, n_t, width), t_at, 1, keepdims=False
    )
    gb_fc1 = lax.dynamic_index_in_dim(
        summed[2 * qv_size : 2 * qv_size + fc1_size].reshape(n_t, fc1_own), t_at, 0, keepdims=False
    )
    gb_out = summed[2 * qv_size + fc1_size : 2 * qv_size + fc1_size + D]
    gb_fc2 = summed[2 * qv_size + fc1_size + D :]
    return (
        output,
        grad_tokens,
        grad_cond,
        g_ada,
        gb_ada,
        g_qkv,
        gb_qv,
        g_out,
        gb_out,
        g_fc1,
        gb_fc1,
        g_fc2,
        gb_fc2,
    )


def solution(mesh):
    specs = (
        P(("dp", "tensor"), None),
        P("dp", None),
        P(("dp", "tensor"), None),
        P("dp", "tensor"),
        P("tensor"),
        P("dp", None, "tensor"),
        P(None, "tensor"),
        P("tensor", "dp"),
        P(),
        P("dp", "tensor"),
        P("tensor"),
        P("tensor", "dp"),
        P(),
    )
    out_specs = (specs[0], specs[0], specs[1]) + specs[3:]
    return jax.shard_map(body, mesh=mesh, in_specs=specs, out_specs=out_specs, check_vma=False)
```
